256 devices in a mesh: blk: 64 (over z, x, y_hi), slab: 4 (over y_lo, core).
Axes of the slice: x: 4, y: 4 (y_hi: 2, y_lo: 2; y = y_hi * 2 + y_lo), z: 8, core: 2. Of those that a mesh axis runs over, the one named last changes fastest.
Arguments:
- a_tiles: bfloat16 [32768, 8192], P('blk', 'slab'), may hold values from -0.125 to 0.125
- tile_cols: int32 [128, 4, 8], P('blk', 'slab'), may hold values from 0 to 15, as said below
- tile_counts: int32 [128, 4], P('blk', 'slab'), may hold values from 1 to 8, as said below
- scaling: float32 [16384], P('slab'), may hold values from 0.1 to 10
- panel: int32 [1], replicated, may hold values from 0 to 127
Outputs:
- normal_band: float32 [32768, 3, 512], P('blk', None, 'slab')
The draws below stay inside these ranges and needn't reach their ends.
Inputs may be any that keep to these rules, and one draw needn't show every extreme that they name: `tile_cols`: the 8 column tiles listed for one row block in one slab are distinct. `tile_counts`: the largest count is 8 in every draw.
All inputs are finite; a program needn't handle non-finite values.
Results may differ from the reference program's by a relative error of at most 0.0015.
Values may be sent and summed in bfloat16 or wider, within the bound.
No kernel may reach another device: no remote copies, remote signals or barrier semaphores. Data moves between devices by JAX's collectives and lax.ppermute only.
A program may use at most 64 MiB of HBM per device.

```python
import math
import jax
import jax.numpy as jnp
from jax import lax

TILE = 256
SLOTS = 8
COL_TILES = 16
RB_DEV = 2
BLOCKS = 128
ROWS = 32768
GROUP_W = 512
COLUMNS = 16384
N_BLK = 64
N_SLAB = 4


def draw_tile_cols(key, part):
    entries = BLOCKS * N_SLAB
    key_list = jax.random.split(jax.random.fold_in(key, 11), entries)
    orders = jax.vmap(lambda single: jax.random.permutation(single, COL_TILES))(key_list)
    return orders[:, :SLOTS].reshape(BLOCKS, N_SLAB, SLOTS).astype(jnp.int32)


def draw_tile_counts(key, part):
    first, second, third = jax.random.split(jax.random.fold_in(key, 23), 3)
    full_rows = jax.random.randint(first, (BLOCKS * N_SLAB,), 0, 20) < 3
    lower_counts = jax.random.randint(second, (BLOCKS * N_SLAB,), 1, SLOTS // 2 + 1)
    counts = jnp.where(full_rows, SLOTS, lower_counts)
    forced = jax.random.randint(third, (), 0, BLOCKS * N_SLAB)
    counts = counts.at[forced].set(SLOTS)
    return counts.reshape(BLOCKS, N_SLAB).astype(jnp.int32)


def levels(stream_key, dims, shards, smallest, largest):
    gain, own = 1.0, jax.random.fold_in(stream_key, 6)
    for position, parts in shards:
        draws = jnp.exp(jax.random.uniform(jax.random.fold_in(own, position), (parts,), jnp.float32, smallest / len(shards), largest / len(shards)))
        gain = gain * jnp.repeat(draws, dims[position] // parts).reshape([-1 if axis == position else 1 for axis in range(len(dims))])
    return gain


def centred(stream_key, shape, deviation, reach, cuts=(), held_as=jnp.bfloat16):
    array = deviation * jax.random.normal(stream_key, shape, jnp.float32)
    if cuts:
        array = array * levels(stream_key, shape, cuts, -0.22, 0.18)
    return jnp.clip(array, -reach, reach).astype(held_as)


def setup_inputs(seed: int = 0) -> dict:
    key_of = jax.random.split(jax.random.key(seed), 6)
    a_tiles = centred(key_of[0], (ROWS, N_SLAB * SLOTS * TILE), (SLOTS * TILE) ** -0.5, 0.125, ((0, 64), (1, 4)))
    tile_cols = draw_tile_cols(jax.random.fold_in(key_of[5], 71), 0)
    tile_counts = draw_tile_counts(jax.random.fold_in(key_of[5], 71), 0)
    scaling = jnp.clip(jnp.exp(math.log(10.0) - 4.6051702 * jax.random.uniform(key_of[3], (COLUMNS,), jnp.float32) ** levels(key_of[3], (COLUMNS,), ((0, 4),), -0.2, 0.2)), 0.1, 10.0)
    panel = jax.random.randint(key_of[4], (1,), 0, BLOCKS).astype(jnp.int32)
    return dict(a_tiles=a_tiles, tile_cols=tile_cols, tile_counts=tile_counts, scaling=scaling, panel=panel)


ridge_shift = 0.05

def reference(a_tiles, tile_cols, tile_counts, scaling, panel):
    blocks_five = a_tiles.reshape(BLOCKS, TILE, N_SLAB, SLOTS, TILE)
    scale_three = scaling.reshape(N_SLAB, COL_TILES, TILE)
    slot_ids = jnp.arange(SLOTS, dtype=jnp.int32)
    slab_ids = jnp.arange(N_SLAB, dtype=jnp.int32)
    live = slot_ids[None, None, :] < tile_counts[:, :, None]
    picked = scale_three[slab_ids[None, :, None], tile_cols]
    picked = jnp.where(live[..., None], picked, jnp.float32(0.0))
    scaled = (blocks_five.astype(jnp.float32) * picked[:, None]).astype(jnp.bfloat16)
    matches = (tile_cols[..., None] == jnp.arange(COL_TILES, dtype=jnp.int32)) & live[..., None]
    found = jnp.any(matches, axis=2).astype(jnp.int32)
    lookup = (jnp.sum(jnp.where(matches, slot_ids[:, None], 0), axis=2) + SLOTS * (1 - found)).astype(jnp.int32)
    padded = jnp.concatenate([blocks_five, jnp.zeros((BLOCKS, TILE, N_SLAB, 1, TILE), jnp.bfloat16)], axis=3)
    member = jnp.arange(RB_DEV, dtype=jnp.int32)
    identity = jnp.eye(TILE, dtype=jnp.float32)

    def one_row(row_block):
        group_pos = row_block // RB_DEV
        own_scaled = scaled[row_block].astype(jnp.float32)
        planes = []
        for shift_by in range(3):
            others = ((group_pos - shift_by) % N_BLK * RB_DEV + member).astype(jnp.int32)
            table = lookup[others]
            slot_index = table[:, slab_ids[:, None], tile_cols[row_block]]
            chosen = padded[others]
            aligned = chosen[member[:, None, None], :, slab_ids[None, :, None], slot_index]
            product = jnp.einsum('xsmy,bsmzy->xbz', own_scaled, aligned.astype(jnp.float32), precision=lax.Precision.HIGHEST)
            if shift_by == 0:
                diag_mask = (member == row_block % RB_DEV).astype(jnp.float32)
                product = product + ridge_shift * identity[:, None, :] * diag_mask[None, :, None]
            planes.append(product.reshape(TILE, GROUP_W))
        return jnp.stack(planes, axis=1)
    band = lax.map(one_row, jnp.arange(BLOCKS, dtype=jnp.int32)).reshape(N_BLK, GROUP_W, 3, GROUP_W)
    pivot_block = panel[0].astype(jnp.int32)
    pivot_group = (pivot_block // RB_DEV).astype(jnp.int32)
    pivot_pos = (pivot_block % RB_DEV).astype(jnp.int32)
    zero_index = jnp.int32(0)
    pivot_offset = (pivot_pos * TILE).astype(jnp.int32)
    row_blocks = jnp.arange(GROUP_W, dtype=jnp.int32) // TILE
    is_pivot = (row_blocks == pivot_pos)[:, None]
    plane_first = band[pivot_group][:, 0, :]
    column_first = lax.dynamic_slice(plane_first, (zero_index, pivot_offset), (GROUP_W, TILE))
    pivot_tile = lax.dynamic_slice(column_first, (pivot_offset, zero_index), (TILE, TILE))
    factor = jnp.linalg.cholesky(pivot_tile)
    solved_first = jax.scipy.linalg.solve_triangular(factor, column_first.T, lower=True).T
    lower_first = jnp.where(is_pivot, jnp.float32(0.0), solved_first)
    plane_first = plane_first - jnp.dot(lower_first.astype(jnp.float32), lower_first.T.astype(jnp.float32), precision=lax.Precision.HIGHEST, preferred_element_type=jnp.float32)
    stacked_factor = jnp.tile(factor, (RB_DEV, 1))
    new_first = jnp.where(is_pivot, stacked_factor, solved_first)
    plane_first = lax.dynamic_update_slice(plane_first, new_first, (zero_index, pivot_offset))
    band = band.at[pivot_group, :, 0, :].set(plane_first)
    return band.reshape(ROWS, 3, GROUP_W)
```

```python
import jax
import jax.numpy as jnp
from jax import lax
from jax.experimental import pallas as pl
from jax.experimental.pallas import tpu as pltpu
from jax.sharding import PartitionSpec as P

ridge_shift = 0.05
AXES = ("blk", "slab")
HIGH = lax.Precision.HIGHEST
SMEM = pl.BlockSpec(memory_space=pltpu.SMEM)
VMEM = pl.BlockSpec(memory_space=pltpu.VMEM)


def product(lhs, rhs, lhs_cols, rhs_cols, scaling, table, scaled, tile, slots, col_tiles, emit):
    for b in range(2):
        for c in range(col_tiles):
            table[b, c] = jnp.int32(slots)
    for b in range(2):
        for n in range(slots):
            col = rhs_cols[b, n]
            table[b, col] = jnp.int32(n)

    def left(t, carry):
        i = t // slots
        m = t % slots
        col = lhs_cols[i, m]
        live = col < col_tiles
        col = jnp.minimum(col, col_tiles - 1)
        other = [table[b, col] for b in range(2)]

        @pl.when(live & ((other[0] < slots) | (other[1] < slots)))
        def _():
            rows = pl.ds(pl.multiple_of(i * tile, tile), tile)
            cols = pl.ds(pl.multiple_of(m * tile, tile), tile)
            scaled[...] = (lhs[rows, cols].astype(jnp.float32) * scaling[pl.ds(col, 1), :]).astype(jnp.bfloat16)
            for b in range(2):

                @pl.when(other[b] < slots)
                def _():
                    cols = pl.ds(pl.multiple_of(other[b] * tile, tile), tile)
                    emit(i, b, lax.dot_general(
                        scaled[...], rhs[b * tile:(b + 1) * tile, cols],
                        (((1,), (1,)), ((), ())), preferred_element_type=jnp.float32))

        return carry

    lax.fori_loop(0, 2 * slots, left, 0)


def own_kernel(tile, slots, col_tiles, cols, scaling, a, far, near, table, scaled):
    y_lo = lax.axis_index("slab") // 2
    far[...] = jnp.zeros_like(far)
    near[...] = jnp.zeros_like(near)

    def emit(i, b, value):
        rows = pl.ds(pl.multiple_of(i * tile, tile), tile)

        @pl.when(b == y_lo)
        def _():
            near[rows, :] += value

        @pl.when(b != y_lo)
        def _():
            far[rows, :] += value

    product(a, a, cols, cols, scaling, table, scaled, tile, slots, col_tiles, emit)


def store_parts(acc, far, near, start):
    y_lo = lax.axis_index("slab") // 2
    size = acc.shape[1]
    far[start:start + size, :] = acc[1 - y_lo].astype(jnp.bfloat16)
    near[start:start + size, :] = acc[y_lo]


def accumulate(acc, tile):
    def emit(i, b, value):
        acc[b, pl.ds(pl.multiple_of(i * tile, tile), tile), :] += value

    return emit


def second_kernel(tile, slots, col_tiles, cols, x_cols, scaling, a, x, far, near, table, scaled, acc):
    core = lax.axis_index("slab") % 2
    acc[...] = jnp.zeros_like(acc)
    emit = accumulate(acc, tile)
    args = (scaling, table, scaled, tile, slots, col_tiles, emit)

    @pl.when(core == 0)
    def _():
        product(a, x, cols, x_cols, *args)

    @pl.when(core == 1)
    def _():
        product(x, a, x_cols, cols, *args)

    store_parts(acc, far, near, 0)


def first_kernel(tile, slots, col_tiles, cols, x_cols, y_cols, scaling, a, x, y, far, near, table, scaled, acc):
    core = lax.axis_index("slab") % 2
    hub = (core + lax.axis_index("blk")) % 2
    emit = accumulate(acc, tile)
    args = (scaling, table, scaled, tile, slots, col_tiles, emit)
    acc[...] = jnp.zeros_like(acc)

    @pl.when((hub == 1) & (core == 0))
    def _():
        product(y, x, y_cols, x_cols, *args)

    @pl.when((hub == 1) & (core == 1))
    def _():
        product(y, a, y_cols, cols, *args)

    store_parts(acc, far, near, 0)
    acc[...] = jnp.zeros_like(acc)

    @pl.when((hub == 1) & (core == 0))
    def _():
        product(a, y, cols, y_cols, *args)

    @pl.when((hub == 1) & (core == 1))
    def _():
        product(x, y, x_cols, y_cols, *args)

    store_parts(acc, far, near, acc.shape[1])


def combine_kernel(near2, got2, near1, got1, cross, ahead, first0, first1, kept):
    core = lax.axis_index("slab") % 2
    rows, width = near2.shape
    half = width // 2
    plane2 = near2[...] + got2[...].astype(jnp.float32)
    plane1 = near1[rows:, :] + got1[rows:, :].astype(jnp.float32)
    other1 = near1[:rows, :] + got1[:rows, :].astype(jnp.float32)
    first0[...] = other1[:, :half].astype(jnp.bfloat16)
    first1[...] = other1[:, half:].astype(jnp.bfloat16)
    for start, value in ((0, plane2), (rows, plane1)):
        mine = jnp.where(core == 0, value[:, :half], value[:, half:])
        theirs = jnp.where(core == 0, value[:, half:], value[:, :half])
        cross[start:start + rows, :] = theirs.astype(jnp.bfloat16)
        ahead[start:start + rows, :] = mine.astype(jnp.bfloat16)
        kept[start:start + rows, :] = mine


def eliminate(matrix, size, group):
    tiles = size // 8
    v = matrix.reshape(tiles, 8, 128)
    ids = lax.broadcasted_iota(jnp.int32, (tiles, 8, 128), 0) * 8 + lax.broadcasted_iota(
        jnp.int32, (tiles, 8, 128), 1)
    pivots = [jnp.ones((8, 128), jnp.float32) for _ in range(tiles)]
    for j in range(0, size, group):
        s = {}
        for a in range(group):
            for b in range(a + 1):
                r = j + a
                s[a, b] = jnp.broadcast_to(v[r // 8, r % 8:r % 8 + 1, j + b:j + b + 1], (8, 128))
        rows = [jnp.broadcast_to(v[(j + a) // 8, (j + a) % 8:(j + a) % 8 + 1, :], (8, 128)) for a in range(group)]
        below = (j + group) // 8
        last = j + group >= size
        cols = [] if last else [
            jnp.broadcast_to(v[below:, :, j + b:j + b + 1], (tiles - below, 8, 128)) for b in range(group)]
        low = {}
        inverse = []
        for b in range(group):
            inverse.append(1.0 / s[b, b])
            for a in range(b + 1, group):
                low[a, b] = s[a, b] * inverse[b]
            for a in range(b + 1, group):
                for c in range(b + 1, a + 1):
                    s[a, c] = s[a, c] - low[a, b] * s[c, b]
        for a in range(group):
            for b in range(a):
                rows[a] = rows[a] - low[a, b] * rows[b]
        top = j // 8
        kept = v[top]
        for a in range(group):
            here = ids[top] == j + a
            kept = jnp.where(here, rows[a], kept)
            pivots[top] = jnp.where(here, s[a, a], pivots[top])
        pieces = [v[:top]] if top else []
        pieces.append(kept[None])
        if not last:
            steps = []
            update = None
            for b in range(group):
                step = cols[b]
                for k in range(b):
                    step = step - steps[k] * s[b, k][None]
                steps.append(step * inverse[b][None])
                term = steps[b] * rows[b][None]
                update = term if update is None else update + term
            pieces.append(v[below:] - update)
        v = jnp.concatenate(pieces, 0) if len(pieces) > 1 else pieces[0]
    return (v * lax.rsqrt(jnp.stack(pivots))).reshape(size, 128)


def panel_factor(w, u, size, group):
    n, width = w.shape
    for start in range(0, n, size):
        base = start // 128 * 128
        square = w[start:start + size, base:base + 128]
        if start > base:
            square = pltpu.roll(square, 128 - (start - base), 1)
        lane = lax.broadcasted_iota(jnp.int32, (size, 128), 1)
        row = lax.broadcasted_iota(jnp.int32, (size, 128), 0)
        square = jnp.where(lane < size, square, jnp.where(lane - size == row, 1.0, 0.0))
        inverse = eliminate(square, size, group)[:, size:2 * size]
        strip = lax.dot_general(
            inverse, w[start:start + size, :], (((1,), (0,)), ((), ())),
            precision=HIGH, preferred_element_type=jnp.float32)
        lane = lax.broadcasted_iota(jnp.int32, (size, width), 1)
        row = lax.broadcasted_iota(jnp.int32, (size, width), 0)
        strip = jnp.where(lane - start >= row, strip, 0.0)
        u[start:start + size, :] = strip
        if start + size < n:
            w[start + size:, :] = w[start + size:, :] - lax.dot_general(
                strip[:, start + size:n], strip, (((0,), (0,)), ((), ())),
                precision=HIGH, preferred_element_type=jnp.float32)


def panel_kernel(tile, panel, part, other, column, lower, total, w, u):
    slab = lax.axis_index("slab")
    core = slab % 2
    y_lo = slab // 2
    half = tile // 2
    block = panel[0]
    pos = block % 2
    holds = (block // 2 == lax.axis_index("blk")) & (pos == y_lo)
    total[...] = part[...] + other[...]
    eye = jnp.where(
        lax.broadcasted_iota(jnp.int32, (tile, tile), 0) == lax.broadcasted_iota(jnp.int32, (tile, tile), 1),
        jnp.float32(ridge_shift), jnp.float32(0.0))
    total[pl.ds(pl.multiple_of(y_lo * tile, tile), tile), :] += eye

    @pl.when(jnp.logical_not(holds))
    def _():
        lower[...] = jnp.zeros_like(lower)

        @pl.when(core == 0)
        def _():
            column[...] = total[:, :half]

        @pl.when(core == 1)
        def _():
            column[...] = total[:, half:]

    @pl.when(holds)
    def _():
        pivot_rows = pl.ds(pl.multiple_of(pos * tile, tile), tile)
        other_rows = pl.ds(pl.multiple_of((1 - pos) * tile, tile), tile)
        square = total[pivot_rows, :]
        w[:, :tile] = (square + square.T) * 0.5
        w[:, tile:] = total[other_rows, :].T
        panel_factor(w, u, 64, 8)
        lower[...] = u[:, tile:].astype(lower.dtype)
        rows = pl.ds(pl.multiple_of(core * half, half), half)
        column[pivot_rows, :] = u[rows, :tile].T
        column[other_rows, :] = u[rows, tile:].T


def final_kernel(tile, panel, column, lower, kept, cross, ahead, first0, first1, out):
    slab = lax.axis_index("slab")
    core = slab % 2
    y_lo = slab // 2
    half = tile // 2
    group = lax.axis_index("blk")
    odd = group % 2
    rows = column.shape[0]
    block = panel[0]
    pos = block % 2
    out[0] = column[...]

    @pl.when((block // 2 == group) & (pos != y_lo))
    def _():
        left = lower[...].astype(jnp.float32)
        right = jnp.where(core == 0, left[:, :half], left[:, half:])
        here = pl.ds(pl.multiple_of(y_lo * tile, tile), tile)
        out[0, here, :] = out[0, here, :] - lax.dot_general(
            left, right, (((0,), (0,)), ((), ())), precision=HIGH, preferred_element_type=jnp.float32)

    wide = lambda ref, start: ref[start:start + rows, :].astype(jnp.float32)

    @pl.when(core == 0)
    def _():
        out[2] = kept[:rows, :] + wide(cross, 0)

        @pl.when(odd == 1)
        def _():
            out[1] = kept[rows:, :] + wide(first0, 0)

        @pl.when(odd == 0)
        def _():
            out[1] = wide(cross, rows) + wide(first0, 0)

    @pl.when(core == 1)
    def _():
        out[2] = wide(ahead, 0) + wide(cross, 0)

        @pl.when(odd == 1)
        def _():
            out[1] = wide(cross, rows) + wide(first1, 0)

        @pl.when(odd == 0)
        def _():
            out[1] = wide(ahead, rows) + wide(first1, 0)


def make_body(groups, slabs):
    devices = [(g, s) for g in range(groups) for s in range(slabs)]
    at = lambda g, s: (g % groups) * slabs + s
    forward = lambda s: s % 2 == 0
    hubs = [(g, s) for g, s in devices if (g + s) % 2 == 1]
    far_pairs = [(at(g, s), at(g + (2 if forward(s) else -2), s)) for g, s in devices]
    near_pairs = [(at(g + (-1 if forward(s) else 1), s), at(g, s)) for g, s in hubs]
    chip_pairs = [(at(g, s), at(g, s ^ 2)) for g, s in devices]
    chip_hub_pairs = [(at(g, s), at(g, s ^ 2)) for g, s in hubs]
    core_pairs = [(at(g, s), at(g, s ^ 1)) for g, s in devices]
    cross_pairs = [(at(g, s), at(g, s + 1) if forward(s) else at(g + 2, s - 1)) for g, s in devices]
    ahead_pairs = [(at(g, s), at(g + 2, s)) for g, s in devices if not forward(s)]
    first0_pairs = [(at(g, s), at(g - 1, s) if forward(s) else at(g + 1, s - 1)) for g, s in hubs]
    first1_pairs = [(at(g, s), at(g - 1, s + 1) if forward(s) else at(g + 1, s)) for g, s in hubs]

    def move(value, pairs):
        return lax.ppermute(value, AXES, pairs)

    def body(a_tiles, tile_cols, tile_counts, scaling, panel):
        rows = a_tiles.shape[0]
        blocks = tile_cols.shape[0]
        slots = tile_cols.shape[2]
        tile = rows // blocks
        col_tiles = scaling.shape[0] // tile
        half = tile // 2
        f32 = jnp.float32
        bf16 = jnp.bfloat16
        shape = jax.ShapeDtypeStruct
        slot_ids = jnp.arange(slots, dtype=jnp.int32)
        cols = jnp.where(slot_ids[None, :] < tile_counts, tile_cols[:, 0, :], col_tiles)
        scales = scaling.reshape(col_tiles, tile)
        x = move(a_tiles, far_pairs)
        y = move(a_tiles, near_pairs)
        x_cols = move(cols, far_pairs)
        y_cols = move(cols, near_pairs)
        table = pltpu.SMEM((2, col_tiles + 1), jnp.int32)
        scaled = pltpu.VMEM((tile, tile), bf16)
        acc = pltpu.VMEM((2, rows, tile), f32)
        sizes = (tile, slots, col_tiles)
        far0, near0 = pl.pallas_call(
            lambda *refs: own_kernel(*sizes, *refs),
            out_shape=(shape((rows, tile), f32), shape((rows, tile), f32)),
            in_specs=[SMEM, VMEM, VMEM], out_specs=(VMEM, VMEM),
            scratch_shapes=[table, scaled], name="plane_zero",
        )(cols, scales, a_tiles)
        part = near0 + move(far0, chip_pairs)
        other = move(part, core_pairs)
        column, lower = pl.pallas_call(
            lambda *refs: panel_kernel(tile, *refs),
            out_shape=(shape((rows, half), f32), shape((tile, tile), bf16)),
            in_specs=[SMEM, VMEM, VMEM], out_specs=(VMEM, VMEM),
            scratch_shapes=[pltpu.VMEM((rows, tile), f32), pltpu.VMEM((tile, rows), f32), pltpu.VMEM((tile, rows), f32)],
            name="panel_step",
        )(panel, part, other)
        lower = move(lower, chip_pairs)
        far2, near2 = pl.pallas_call(
            lambda *refs: second_kernel(*sizes, *refs),
            out_shape=(shape((rows, tile), bf16), shape((rows, tile), f32)),
            in_specs=[SMEM, SMEM, VMEM, VMEM, VMEM], out_specs=(VMEM, VMEM),
            scratch_shapes=[table, scaled, acc], name="plane_two",
        )(cols, x_cols, scales, a_tiles, x)
        got2 = move(far2, chip_pairs)
        far1, near1 = pl.pallas_call(
            lambda *refs: first_kernel(*sizes, *refs),
            out_shape=(shape((2 * rows, tile), bf16), shape((2 * rows, tile), f32)),
            in_specs=[SMEM, SMEM, SMEM, VMEM, VMEM, VMEM, VMEM], out_specs=(VMEM, VMEM),
            scratch_shapes=[table, scaled, acc], name="plane_one",
        )(cols, x_cols, y_cols, scales, a_tiles, x, y)
        got1 = move(far1, chip_hub_pairs)
        cross, ahead, first0, first1, kept = pl.pallas_call(
            combine_kernel,
            out_shape=(shape((2 * rows, half), bf16), shape((2 * rows, half), bf16), shape((rows, half), bf16),
                       shape((rows, half), bf16), shape((2 * rows, half), f32)),
            in_specs=[VMEM] * 4, out_specs=(VMEM,) * 5, name="combine",
        )(near2, got2, near1, got1)
        cross = move(cross, cross_pairs)
        ahead = move(ahead, ahead_pairs)
        first0 = move(first0, first0_pairs)
        first1 = move(first1, first1_pairs)
        out = pl.pallas_call(
            lambda *refs: final_kernel(tile, *refs),
            out_shape=shape((3, rows, half), f32),
            in_specs=[SMEM] + [VMEM] * 7, out_specs=VMEM, name="assemble",
        )(panel, column, lower, kept, cross, ahead, first0, first1)
        return out.transpose(1, 0, 2)

    return body


def solution(mesh):
    return jax.shard_map(
        make_body(mesh.shape["blk"], mesh.shape["slab"]),
        mesh=mesh,
        in_specs=(P("blk", "slab"), P("blk", "slab", None), P("blk", "slab"), P("slab"), P()),
        out_specs=P("blk", None, "slab"),
        check_vma=False,
    )
```

```python
import jax
import jax.numpy as jnp
from jax import lax
from jax.experimental import pallas as pl
from jax.experimental.pallas import tpu as pltpu
from jax.sharding import PartitionSpec as P

ridge_shift = 0.05
AXES = ("blk", "slab")
HIGH = lax.Precision.HIGHEST
SMEM = pl.BlockSpec(memory_space=pltpu.SMEM)
ANY = pl.BlockSpec(memory_space=pl.ANY)
VMEM = pl.BlockSpec(memory_space=pltpu.VMEM)


def product(lhs, rhs, lhs_cols, rhs_cols, scaling, table, scaled, tile, slots, col_tiles, emit):
    for b in range(2):
        for c in range(col_tiles):
            table[b, c] = jnp.int32(slots)
    for b in range(2):
        for n in range(slots):
            col = rhs_cols[b, n]
            table[b, col] = jnp.int32(n)

    def left(t, carry):
        i = t // slots
        m = t % slots
        col = lhs_cols[i, m]
        live = col < col_tiles
        col = jnp.minimum(col, col_tiles - 1)
        other = [table[b, col] for b in range(2)]

        @pl.when(live & ((other[0] < slots) | (other[1] < slots)))
        def _():
            rows = pl.ds(pl.multiple_of(i * tile, tile), tile)
            cols = pl.ds(pl.multiple_of(m * tile, tile), tile)
            scaled[...] = (lhs[rows, cols].astype(jnp.float32) * scaling[pl.ds(col, 1), :]).astype(jnp.bfloat16)
            for b in range(2):

                @pl.when(other[b] < slots)
                def _():
                    cols = pl.ds(pl.multiple_of(other[b] * tile, tile), tile)
                    emit(i, b, lax.dot_general(
                        scaled[...], rhs[b * tile:(b + 1) * tile, cols],
                        (((1,), (1,)), ((), ())), preferred_element_type=jnp.float32))

        return carry

    lax.fori_loop(0, 2 * slots, left, 0)


def own_kernel(tile, slots, col_tiles, cols, scaling, a, give, keep, table, scaled, acc):
    slab = lax.axis_index("slab")
    core = slab % 2
    y_lo = slab // 2
    rows = acc.shape[1]
    acc[...] = jnp.zeros_like(acc)

    def emit(i, b, value):
        acc[b, pl.ds(pl.multiple_of(i * tile, tile), tile), :] += value

    product(a, a, cols, cols, scaling, table, scaled, tile, slots, col_tiles, emit)
    give[:rows, :] = acc[y_lo]
    keep[:rows, :] = acc[y_lo]
    give[rows:, :] = acc[1 - y_lo, pl.ds(pl.multiple_of((1 - core) * tile, tile), tile), :]
    keep[rows:, :] = acc[1 - y_lo, pl.ds(pl.multiple_of(core * tile, tile), tile), :]


def fetch(copies, sems):
    started = [pltpu.make_async_copy(src, dst, sems.at[n]) for n, (src, dst) in enumerate(copies)]
    for copy in started:
        copy.start()
    return started


def other_kernel(tile, slots, col_tiles, cols, x_cols, y_cols, scaling, a_any, x_any, y_any, p1, p2, p3, kept2,
                 q1, q2, q3, kept1, a, x, y, table, scaled, acc, sems):
    slab = lax.axis_index("slab")
    core = slab % 2
    hub = (core + lax.axis_index("blk")) % 2 == 1
    rows = a.shape[0]
    half = tile // 2
    copies = fetch([(a_any, a), (x_any, x)], sems)
    third = pltpu.make_async_copy(y_any, y, sems.at[2])

    @pl.when(hub)
    def _():
        third.start()

    def emit(i, b, value):
        at = pl.ds(pl.multiple_of(i * tile, tile), tile)
        acc[2 * b, at, :] += value[:, :half]
        acc[2 * b + 1, at, :] += value[:, half:]

    args = (scaling, table, scaled, tile, slots, col_tiles, emit)
    acc[...] = jnp.zeros_like(acc)
    for copy in copies:
        copy.wait()

    @pl.when(core == 0)
    def _():
        product(a, x, cols, x_cols, *args)

    @pl.when(core == 1)
    def _():
        product(x, a, x_cols, cols, *args)

    kept2[...] = acc[slab]
    for k, ref in ((1, p1), (2, p2), (3, p3)):
        ref[...] = acc[slab ^ k].astype(ref.dtype)

    def store(start):
        kept1[start:start + rows, :] = acc[slab]
        for k, ref in ((1, q1), (2, q2), (3, q3)):
            ref[start:start + rows, :] = acc[slab ^ k].astype(ref.dtype)

    @pl.when(jnp.logical_not(hub))
    def _():
        kept1[...] = jnp.zeros_like(kept1)

    @pl.when(hub)
    def _():
        acc[...] = jnp.zeros_like(acc)
        third.wait()

        @pl.when(core == 0)
        def _():
            product(y, x, y_cols, x_cols, *args)

        @pl.when(core == 1)
        def _():
            product(y, a, y_cols, cols, *args)

        store(0)
        acc[...] = jnp.zeros_like(acc)

        @pl.when(core == 0)
        def _():
            product(a, y, cols, y_cols, *args)

        @pl.when(core == 1)
        def _():
            product(x, y, x_cols, y_cols, *args)

        store(rows)


def combine_kernel(k2, r1, r2, r3, k1, t1, t2, t3, ahead, beside, own2, own1, v2, u1, u2, u3, v1, w1, w2, w3, sems):
    core = lax.axis_index("slab") % 2
    pairs = [(k2, v2), (r1, u1), (r2, u2), (r3, u3), (k1, v1), (t1, w1), (t2, w2), (t3, w3)]
    copies = fetch(pairs, sems)
    rows = k2.shape[0]
    wide = lambda ref: ref[...].astype(jnp.float32)
    for copy in copies[:4]:
        copy.wait()
    same = v2[...] + wide(u2)
    swapped = wide(u1) + wide(u3)
    own2[...] = jnp.where(core == 0, same, swapped)
    ahead[:rows, :] = jnp.where(core == 0, swapped, same).astype(ahead.dtype)
    for copy in copies[4:]:
        copy.wait()
    plane1 = v1[...] + wide(w1) + wide(w2) + wide(w3)
    beside[...] = plane1[:rows].astype(beside.dtype)
    ahead[rows:, :] = plane1[rows:].astype(ahead.dtype)
    own1[...] = plane1[rows:]


def eliminate(matrix, size, group):
    tiles = size // 8
    v = matrix.reshape(tiles, 8, 128)
    ids = lax.broadcasted_iota(jnp.int32, (tiles, 8, 128), 0) * 8 + lax.broadcasted_iota(
        jnp.int32, (tiles, 8, 128), 1)
    pivots = [jnp.ones((8, 128), jnp.float32) for _ in range(tiles)]
    for j in range(0, size, group):
        s = {}
        for a in range(group):
            for b in range(a + 1):
                r = j + a
                s[a, b] = jnp.broadcast_to(v[r // 8, r % 8:r % 8 + 1, j + b:j + b + 1], (8, 128))
        rows = [jnp.broadcast_to(v[(j + a) // 8, (j + a) % 8:(j + a) % 8 + 1, :], (8, 128)) for a in range(group)]
        below = (j + group) // 8
        last = j + group >= size
        cols = [] if last else [
            jnp.broadcast_to(v[below:, :, j + b:j + b + 1], (tiles - below, 8, 128)) for b in range(group)]
        low = {}
        inverse = []
        for b in range(group):
            inverse.append(1.0 / s[b, b])
            for a in range(b + 1, group):
                low[a, b] = s[a, b] * inverse[b]
            for a in range(b + 1, group):
                for c in range(b + 1, a + 1):
                    s[a, c] = s[a, c] - low[a, b] * s[c, b]
        for a in range(group):
            for b in range(a):
                rows[a] = rows[a] - low[a, b] * rows[b]
        top = j // 8
        kept = v[top]
        for a in range(group):
            here = ids[top] == j + a
            kept = jnp.where(here, rows[a], kept)
            pivots[top] = jnp.where(here, s[a, a], pivots[top])
        pieces = [v[:top]] if top else []
        pieces.append(kept[None])
        if not last:
            steps = []
            update = None
            for b in range(group):
                step = cols[b]
                for k in range(b):
                    step = step - steps[k] * s[b, k][None]
                steps.append(step * inverse[b][None])
                term = steps[b] * rows[b][None]
                update = term if update is None else update + term
            pieces.append(v[below:] - update)
        v = jnp.concatenate(pieces, 0) if len(pieces) > 1 else pieces[0]
    return (v * lax.rsqrt(jnp.stack(pivots))).reshape(size, 128)


def panel_factor(w, u, size, group):
    n, width = w.shape
    for start in range(0, n, size):
        base = start // 128 * 128
        square = w[start:start + size, base:base + 128]
        if start > base:
            square = pltpu.roll(square, 128 - (start - base), 1)
        lane = lax.broadcasted_iota(jnp.int32, (size, 128), 1)
        row = lax.broadcasted_iota(jnp.int32, (size, 128), 0)
        square = jnp.where(lane < size, square, jnp.where(lane - size == row, 1.0, 0.0))
        inverse = eliminate(square, size, group)[:, size:2 * size]
        strip = lax.dot_general(
            inverse, w[start:start + size, :], (((1,), (0,)), ((), ())),
            precision=HIGH, preferred_element_type=jnp.float32)
        lane = lax.broadcasted_iota(jnp.int32, (size, width), 1)
        row = lax.broadcasted_iota(jnp.int32, (size, width), 0)
        strip = jnp.where(lane - start >= row, strip, 0.0)
        u[start:start + size, :] = strip
        if start + size < n:
            w[start + size:, :] = w[start + size:, :] - lax.dot_general(
                strip[:, start + size:n], strip, (((0,), (0,)), ((), ())),
                precision=HIGH, preferred_element_type=jnp.float32)


def panel_kernel(tile, panel, keep, got, mine, theirs, column, lower, total, w, u):
    slab = lax.axis_index("slab")
    core = slab % 2
    y_lo = slab // 2
    half = tile // 2
    block = panel[0]
    pos = block % 2
    holds = (block // 2 == lax.axis_index("blk")) & (pos == y_lo)
    rows = total.shape[0]
    total[...] = keep[:rows, :] + got[:rows, :]
    total[pl.ds(pl.multiple_of(core * tile, tile), tile), :] += mine[...]
    total[pl.ds(pl.multiple_of((1 - core) * tile, tile), tile), :] += theirs[...]
    eye = jnp.where(
        lax.broadcasted_iota(jnp.int32, (tile, tile), 0) == lax.broadcasted_iota(jnp.int32, (tile, tile), 1),
        jnp.float32(ridge_shift), jnp.float32(0.0))
    total[pl.ds(pl.multiple_of(y_lo * tile, tile), tile), :] += eye

    @pl.when(jnp.logical_not(holds))
    def _():
        lower[...] = jnp.zeros_like(lower)

        @pl.when(core == 0)
        def _():
            column[...] = total[:, :half]

        @pl.when(core == 1)
        def _():
            column[...] = total[:, half:]

    @pl.when(holds)
    def _():
        pivot_rows = pl.ds(pl.multiple_of(pos * tile, tile), tile)
        other_rows = pl.ds(pl.multiple_of((1 - pos) * tile, tile), tile)
        square = total[pivot_rows, :]
        w[:, :tile] = (square + square.T) * 0.5
        w[:, tile:] = total[other_rows, :].T
        panel_factor(w, u, 64, 8)
        lower[...] = u[:, tile:].astype(lower.dtype)
        rows = pl.ds(pl.multiple_of(core * half, half), half)
        column[pivot_rows, :] = u[rows, :tile].T
        column[other_rows, :] = u[rows, tile:].T


def final_kernel(tile, panel, column, lower, own2, own1, ahead, beside, out):
    slab = lax.axis_index("slab")
    core = slab % 2
    y_lo = slab // 2
    half = tile // 2
    group = lax.axis_index("blk")
    rows = column.shape[0]
    block = panel[0]
    pos = block % 2
    out[0] = column[...]

    @pl.when((block // 2 == group) & (pos != y_lo))
    def _():
        left = lower[...].astype(jnp.float32)
        right = jnp.where(core == 0, left[:, :half], left[:, half:])
        here = pl.ds(pl.multiple_of(y_lo * tile, tile), tile)
        out[0, here, :] = out[0, here, :] - lax.dot_general(
            left, right, (((0,), (0,)), ((), ())), precision=HIGH, preferred_element_type=jnp.float32)

    out[2] = own2[...] + ahead[:rows, :].astype(jnp.float32)
    late = jnp.where(group % 2 == 1, own1[...], ahead[rows:, :].astype(jnp.float32))
    out[1] = late + beside[...].astype(jnp.float32)


def make_body(groups, slabs):
    devices = [(g, s) for g in range(groups) for s in range(slabs)]
    at = lambda g, s: (g % groups) * slabs + s
    forward = lambda s: s % 2 == 0
    hubs = [(g, s) for g, s in devices if (g + s) % 2 == 1]
    far_pairs = [(at(g, s), at(g + (2 if forward(s) else -2), s)) for g, s in devices]
    near_pairs = [(at(g + (-1 if forward(s) else 1), s), at(g, s)) for g, s in hubs]
    slab_pairs = lambda k, among=devices: [(at(g, s), at(g, s ^ k)) for g, s in among]
    ahead_pairs = [(at(g, s), at(g + 2, s)) for g, s in devices]
    beside_pairs = [(at(g, s), at(g ^ 1, s)) for g, s in devices]

    def move(value, pairs):
        return lax.ppermute(value, AXES, pairs)

    def body(a_tiles, tile_cols, tile_counts, scaling, panel):
        rows = a_tiles.shape[0]
        blocks = tile_cols.shape[0]
        slots = tile_cols.shape[2]
        tile = rows // blocks
        col_tiles = scaling.shape[0] // tile
        half = tile // 2
        f32 = jnp.float32
        bf16 = jnp.bfloat16
        shape = jax.ShapeDtypeStruct
        slot_ids = jnp.arange(slots, dtype=jnp.int32)
        cols = jnp.where(slot_ids[None, :] < tile_counts, tile_cols[:, 0, :], col_tiles)
        scales = scaling.reshape(col_tiles, tile)
        x = move(a_tiles, far_pairs)
        y = move(a_tiles, near_pairs)
        x_cols = move(cols, far_pairs)
        y_cols = move(cols, near_pairs)
        table = pltpu.SMEM((2, col_tiles + 1), jnp.int32)
        scaled = pltpu.VMEM((tile, tile), bf16)
        sizes = (tile, slots, col_tiles)
        give, keep = pl.pallas_call(
            lambda *refs: own_kernel(*sizes, *refs),
            out_shape=(shape((rows + tile, tile), f32), shape((rows + tile, tile), f32)),
            in_specs=[SMEM, VMEM, VMEM], out_specs=(VMEM, VMEM),
            scratch_shapes=[table, scaled, pltpu.VMEM((2, rows, tile), f32)], name="plane_zero",
        )(cols, scales, a_tiles)
        got = move(give, slab_pairs(1))
        mine = move(keep[rows:] + got[rows:], slab_pairs(2))
        x, y, mine = lax.optimization_barrier((x, y, mine))
        part = shape((rows, half), bf16)
        two = shape((2 * rows, half), bf16)
        p1, p2, p3, kept2, q1, q2, q3, kept1 = pl.pallas_call(
            lambda *refs: other_kernel(*sizes, *refs),
            out_shape=(part, part, part, shape((rows, half), f32), two, two, two, shape((2 * rows, half), f32)),
            in_specs=[SMEM, SMEM, SMEM, VMEM, ANY, ANY, ANY], out_specs=(VMEM,) * 8,
            scratch_shapes=[pltpu.VMEM(a_tiles.shape, bf16)] * 3 + [
                table, scaled, pltpu.VMEM((4, rows, half), f32), pltpu.SemaphoreType.DMA((3,))],
            name="planes_one_two",
        )(cols, x_cols, y_cols, scales, a_tiles, x, y)
        r2, t2 = move(p2, slab_pairs(2)), move(q2, slab_pairs(2, hubs))
        r3, t3 = move(p3, slab_pairs(3)), move(q3, slab_pairs(3, hubs))
        r1, t1 = move(p1, slab_pairs(1)), move(q1, slab_pairs(1, hubs))
        mine, kept2 = lax.optimization_barrier((mine, kept2))
        theirs = move(mine, slab_pairs(1))
        theirs, kept2 = lax.optimization_barrier((theirs, kept2))
        column, lower = pl.pallas_call(
            lambda *refs: panel_kernel(tile, *refs),
            out_shape=(shape((rows, half), f32), shape((tile, tile), bf16)),
            in_specs=[SMEM] + [VMEM] * 4, out_specs=(VMEM, VMEM),
            scratch_shapes=[pltpu.VMEM((rows, tile), f32), pltpu.VMEM((tile, rows), f32), pltpu.VMEM((tile, rows), f32)],
            name="panel_step",
        )(panel, keep, got, mine, theirs)
        kept2, lower = lax.optimization_barrier((kept2, lower))
        lower = move(lower, slab_pairs(2))
        parts = (kept2, r1, r2, r3, kept1, t1, t2, t3)
        ahead, beside, own2, own1 = pl.pallas_call(
            combine_kernel,
            out_shape=(two, part, shape((rows, half), f32), shape((rows, half), f32)),
            in_specs=[ANY] * 8, out_specs=(VMEM,) * 4,
            scratch_shapes=[pltpu.VMEM(v.shape, v.dtype) for v in parts] + [pltpu.SemaphoreType.DMA((8,))],
            name="combine",
        )(*parts)
        beside = move(beside, beside_pairs)
        ahead = move(ahead, ahead_pairs)
        out = pl.pallas_call(
            lambda *refs: final_kernel(tile, *refs),
            out_shape=shape((3, rows, half), f32),
            in_specs=[SMEM] + [VMEM] * 6, out_specs=VMEM, name="assemble",
        )(panel, column, lower, own2, own1, ahead, beside)
        return out.transpose(1, 0, 2)

    return body


def solution(mesh):
    return jax.shard_map(
        make_body(mesh.shape["blk"], mesh.shape["slab"]),
        mesh=mesh,
        in_specs=(P("blk", "slab"), P("blk", "slab", None), P("blk", "slab"), P("slab"), P()),
        out_specs=P("blk", None, "slab"),
        check_vma=False,
    )
```

```python
import jax
import jax.numpy as jnp
from jax import lax
from jax.experimental import pallas as pl
from jax.experimental.pallas import tpu as pltpu
from jax.sharding import PartitionSpec as P

ridge_shift = 0.05
AXES = ("blk", "slab")
HIGH = lax.Precision.HIGHEST
SMEM = pl.BlockSpec(memory_space=pltpu.SMEM)
ANY = pl.BlockSpec(memory_space=pl.ANY)
VMEM = pl.BlockSpec(memory_space=pltpu.VMEM)


def product(lhs, rhs, lhs_cols, rhs_cols, scaling, table, scaled, tile, slots, col_tiles, emit):
    for b in range(2):
        for c in range(col_tiles):
            table[b, c] = jnp.int32(slots)
    for b in range(2):
        for n in range(slots):
            col = rhs_cols[b, n]
            table[b, col] = jnp.int32(n)

    def left(t, carry):
        i = t // slots
        m = t % slots
        col = lhs_cols[i, m]
        live = col < col_tiles
        col = jnp.minimum(col, col_tiles - 1)
        other = [table[b, col] for b in range(2)]

        @pl.when(live & ((other[0] < slots) | (other[1] < slots)))
        def _():
            rows = pl.ds(pl.multiple_of(i * tile, tile), tile)
            cols = pl.ds(pl.multiple_of(m * tile, tile), tile)
            scaled[...] = (lhs[rows, cols].astype(jnp.float32) * scaling[pl.ds(col, 1), :]).astype(jnp.bfloat16)
            for b in range(2):

                @pl.when(other[b] < slots)
                def _():
                    cols = pl.ds(pl.multiple_of(other[b] * tile, tile), tile)
                    emit(i, b, lax.dot_general(
                        scaled[...], rhs[b * tile:(b + 1) * tile, cols],
                        (((1,), (1,)), ((), ())), preferred_element_type=jnp.float32))

        return carry

    lax.fori_loop(0, 2 * slots, left, 0)


def own_kernel(tile, slots, col_tiles, cols, scaling, a, give, keep, table, scaled, acc):
    slab = lax.axis_index("slab")
    core = slab % 2
    y_lo = slab // 2
    rows = acc.shape[1]
    acc[...] = jnp.zeros_like(acc)

    def emit(i, b, value):
        acc[b, pl.ds(pl.multiple_of(i * tile, tile), tile), :] += value

    product(a, a, cols, cols, scaling, table, scaled, tile, slots, col_tiles, emit)
    give[:rows, :] = acc[y_lo]
    keep[:rows, :] = acc[y_lo]
    give[rows:, :] = acc[1 - y_lo, pl.ds(pl.multiple_of((1 - core) * tile, tile), tile), :]
    keep[rows:, :] = acc[1 - y_lo, pl.ds(pl.multiple_of(core * tile, tile), tile), :]


def fetch(copies, sems):
    started = [pltpu.make_async_copy(src, dst, sems.at[n]) for n, (src, dst) in enumerate(copies)]
    for copy in started:
        copy.start()
    return started


def adder(acc, tile):
    half = tile // 2

    def emit(i, b, value):
        at = pl.ds(pl.multiple_of(i * tile, tile), tile)
        acc[2 * b, at, :] += value[:, :half]
        acc[2 * b + 1, at, :] += value[:, half:]

    return emit


def second_kernel(tile, slots, col_tiles, cols, x_cols, scaling, a_any, x_any, p1, p2, p3, kept,
                  a, x, table, scaled, acc, sems):
    slab = lax.axis_index("slab")
    core = slab % 2
    copies = fetch([(a_any, a), (x_any, x)], sems)
    args = (scaling, table, scaled, tile, slots, col_tiles, adder(acc, tile))
    acc[...] = jnp.zeros_like(acc)
    for copy in copies:
        copy.wait()

    @pl.when(core == 0)
    def _():
        product(a, x, cols, x_cols, *args)

    @pl.when(core == 1)
    def _():
        product(x, a, x_cols, cols, *args)

    kept[...] = acc[slab]
    for k, ref in ((1, p1), (2, p2), (3, p3)):
        ref[...] = acc[slab ^ k].astype(ref.dtype)


def first_kernel(tile, slots, col_tiles, cols, x_cols, y_cols, scaling, a_any, x_any, y_any, q1, q2, q3, kept,
                 a, x, y, table, scaled, acc, sems):
    slab = lax.axis_index("slab")
    core = slab % 2
    hub = (core + lax.axis_index("blk")) % 2 == 1
    rows = a.shape[0]

    def store(start):
        kept[start:start + rows, :] = acc[slab]
        for k, ref in ((1, q1), (2, q2), (3, q3)):
            ref[start:start + rows, :] = acc[slab ^ k].astype(ref.dtype)

    @pl.when(jnp.logical_not(hub))
    def _():
        for ref in (q1, q2, q3, kept):
            ref[...] = jnp.zeros_like(ref)

    @pl.when(hub)
    def _():
        copies = fetch([(y_any, y), (x_any, x), (a_any, a)], sems)
        args = (scaling, table, scaled, tile, slots, col_tiles, adder(acc, tile))
        acc[...] = jnp.zeros_like(acc)
        for copy in copies:
            copy.wait()

        @pl.when(core == 0)
        def _():
            product(y, x, y_cols, x_cols, *args)

        @pl.when(core == 1)
        def _():
            product(y, a, y_cols, cols, *args)

        store(0)
        acc[...] = jnp.zeros_like(acc)

        @pl.when(core == 0)
        def _():
            product(a, y, cols, y_cols, *args)

        @pl.when(core == 1)
        def _():
            product(x, y, x_cols, y_cols, *args)

        store(rows)


def eliminate(matrix, size, group):
    tiles = size // 8
    v = matrix.reshape(tiles, 8, 128)
    ids = lax.broadcasted_iota(jnp.int32, (tiles, 8, 128), 0) * 8 + lax.broadcasted_iota(
        jnp.int32, (tiles, 8, 128), 1)
    pivots = [jnp.ones((8, 128), jnp.float32) for _ in range(tiles)]
    for j in range(0, size, group):
        s = {}
        for a in range(group):
            for b in range(a + 1):
                r = j + a
                s[a, b] = jnp.broadcast_to(v[r // 8, r % 8:r % 8 + 1, j + b:j + b + 1], (8, 128))
        rows = [jnp.broadcast_to(v[(j + a) // 8, (j + a) % 8:(j + a) % 8 + 1, :], (8, 128)) for a in range(group)]
        below = (j + group) // 8
        last = j + group >= size
        cols = [] if last else [
            jnp.broadcast_to(v[below:, :, j + b:j + b + 1], (tiles - below, 8, 128)) for b in range(group)]
        low = {}
        inverse = []
        for b in range(group):
            inverse.append(1.0 / s[b, b])
            for a in range(b + 1, group):
                low[a, b] = s[a, b] * inverse[b]
            for a in range(b + 1, group):
                for c in range(b + 1, a + 1):
                    s[a, c] = s[a, c] - low[a, b] * s[c, b]
        for a in range(group):
            for b in range(a):
                rows[a] = rows[a] - low[a, b] * rows[b]
        top = j // 8
        kept = v[top]
        for a in range(group):
            here = ids[top] == j + a
            kept = jnp.where(here, rows[a], kept)
            pivots[top] = jnp.where(here, s[a, a], pivots[top])
        pieces = [v[:top]] if top else []
        pieces.append(kept[None])
        if not last:
            steps = []
            update = None
            for b in range(group):
                step = cols[b]
                for k in range(b):
                    step = step - steps[k] * s[b, k][None]
                steps.append(step * inverse[b][None])
                term = steps[b] * rows[b][None]
                update = term if update is None else update + term
            pieces.append(v[below:] - update)
        v = jnp.concatenate(pieces, 0) if len(pieces) > 1 else pieces[0]
    return (v * lax.rsqrt(jnp.stack(pivots))).reshape(size, 128)


def panel_factor(w, u, size, group):
    n, width = w.shape
    for start in range(0, n, size):
        base = start // 128 * 128
        square = w[start:start + size, base:base + 128]
        if start > base:
            square = pltpu.roll(square, 128 - (start - base), 1)
        lane = lax.broadcasted_iota(jnp.int32, (size, 128), 1)
        row = lax.broadcasted_iota(jnp.int32, (size, 128), 0)
        square = jnp.where(lane < size, square, jnp.where(lane - size == row, 1.0, 0.0))
        inverse = eliminate(square, size, group)[:, size:2 * size]
        strip = lax.dot_general(
            inverse, w[start:start + size, :], (((1,), (0,)), ((), ())),
            precision=HIGH, preferred_element_type=jnp.float32)
        lane = lax.broadcasted_iota(jnp.int32, (size, width), 1)
        row = lax.broadcasted_iota(jnp.int32, (size, width), 0)
        strip = jnp.where(lane - start >= row, strip, 0.0)
        u[start:start + size, :] = strip
        if start + size < n:
            w[start + size:, :] = w[start + size:, :] - lax.dot_general(
                strip[:, start + size:n], strip, (((0,), (0,)), ((), ())),
                precision=HIGH, preferred_element_type=jnp.float32)


def panel_kernel(tile, panel, keep, got, mine, theirs, column, lower, total, w, u):
    slab = lax.axis_index("slab")
    core = slab % 2
    y_lo = slab // 2
    half = tile // 2
    block = panel[0]
    pos = block % 2
    holds = (block // 2 == lax.axis_index("blk")) & (pos == y_lo)
    rows = total.shape[0]
    total[...] = keep[:rows, :] + got[:rows, :]
    total[pl.ds(pl.multiple_of(core * tile, tile), tile), :] += mine[...]
    total[pl.ds(pl.multiple_of((1 - core) * tile, tile), tile), :] += theirs[...]
    eye = jnp.where(
        lax.broadcasted_iota(jnp.int32, (tile, tile), 0) == lax.broadcasted_iota(jnp.int32, (tile, tile), 1),
        jnp.float32(ridge_shift), jnp.float32(0.0))
    total[pl.ds(pl.multiple_of(y_lo * tile, tile), tile), :] += eye

    @pl.when(jnp.logical_not(holds))
    def _():
        lower[...] = jnp.zeros_like(lower)

        @pl.when(core == 0)
        def _():
            column[...] = total[:, :half]

        @pl.when(core == 1)
        def _():
            column[...] = total[:, half:]

    @pl.when(holds)
    def _():
        pivot_rows = pl.ds(pl.multiple_of(pos * tile, tile), tile)
        other_rows = pl.ds(pl.multiple_of((1 - pos) * tile, tile), tile)
        square = total[pivot_rows, :]
        w[:, :tile] = (square + square.T) * 0.5
        w[:, tile:] = total[other_rows, :].T
        panel_factor(w, u, 64, 8)
        lower[...] = u[:, tile:].astype(lower.dtype)
        rows = pl.ds(pl.multiple_of(core * half, half), half)
        column[pivot_rows, :] = u[rows, :tile].T
        column[other_rows, :] = u[rows, tile:].T


def final_kernel(tile, panel, column, lower, own2, own1, ahead2, ahead1, beside, out):
    slab = lax.axis_index("slab")
    core = slab % 2
    y_lo = slab // 2
    half = tile // 2
    group = lax.axis_index("blk")
    rows = column.shape[0]
    block = panel[0]
    pos = block % 2
    out[0] = column[...]

    @pl.when((block // 2 == group) & (pos != y_lo))
    def _():
        left = lower[...].astype(jnp.float32)
        right = jnp.where(core == 0, left[:, :half], left[:, half:])
        here = pl.ds(pl.multiple_of(y_lo * tile, tile), tile)
        out[0, here, :] = out[0, here, :] - lax.dot_general(
            left, right, (((0,), (0,)), ((), ())), precision=HIGH, preferred_element_type=jnp.float32)

    out[2] = own2[...] + ahead2[...].astype(jnp.float32)
    late = jnp.where(group % 2 == 1, own1[...], ahead1[...].astype(jnp.float32))
    out[1] = late + beside[...].astype(jnp.float32)


def make_body(groups, slabs):
    devices = [(g, s) for g in range(groups) for s in range(slabs)]
    at = lambda g, s: (g % groups) * slabs + s
    forward = lambda s: s % 2 == 0
    hubs = [(g, s) for g, s in devices if (g + s) % 2 == 1]
    far_pairs = [(at(g, s), at(g + (2 if forward(s) else -2), s)) for g, s in devices]
    near_pairs = [(at(g + (-1 if forward(s) else 1), s), at(g, s)) for g, s in hubs]
    slab_pairs = lambda k, among=devices: [(at(g, s), at(g, s ^ k)) for g, s in among]
    ahead_pairs = [(at(g, s), at(g + 2, s)) for g, s in devices]
    even_ahead_pairs = [(at(g, s), at(g + 2, s)) for g, s in devices if g % 2 == 0]
    beside_pairs = [(at(g, s), at(g ^ 1, s)) for g, s in devices]

    hold = lax.optimization_barrier

    def move(value, pairs):
        return lax.ppermute(value, AXES, pairs)

    def body(a_tiles, tile_cols, tile_counts, scaling, panel):
        rows = a_tiles.shape[0]
        blocks = tile_cols.shape[0]
        slots = tile_cols.shape[2]
        tile = rows // blocks
        col_tiles = scaling.shape[0] // tile
        half = tile // 2
        f32 = jnp.float32
        bf16 = jnp.bfloat16
        shape = jax.ShapeDtypeStruct
        slot_ids = jnp.arange(slots, dtype=jnp.int32)
        cols = jnp.where(slot_ids[None, :] < tile_counts, tile_cols[:, 0, :], col_tiles)
        scales = scaling.reshape(col_tiles, tile)
        x_cols = move(cols, far_pairs)
        y_cols = move(cols, near_pairs)
        x = move(a_tiles, far_pairs)
        y = move(a_tiles, near_pairs)
        table = pltpu.SMEM((2, col_tiles + 1), jnp.int32)
        scaled = pltpu.VMEM((tile, tile), bf16)
        sizes = (tile, slots, col_tiles)
        give, keep = pl.pallas_call(
            lambda *refs: own_kernel(*sizes, *refs),
            out_shape=(shape((rows + tile, tile), f32), shape((rows + tile, tile), f32)),
            in_specs=[SMEM, VMEM, VMEM], out_specs=(VMEM, VMEM),
            scratch_shapes=[table, scaled, pltpu.VMEM((2, rows, tile), f32)], name="plane_zero",
        )(cols, scales, a_tiles)
        got = move(give, slab_pairs(1))
        got, x_cols, y_cols = hold((got, x_cols, y_cols))
        mine = move(keep[rows:] + got[rows:], slab_pairs(2))
        part = shape((rows, half), bf16)
        two = shape((2 * rows, half), bf16)
        whole = pltpu.VMEM(a_tiles.shape, bf16)
        acc = pltpu.VMEM((4, rows, half), f32)
        p1, p2, p3, kept2 = pl.pallas_call(
            lambda *refs: second_kernel(*sizes, *refs),
            out_shape=(part, part, part, shape((rows, half), f32)),
            in_specs=[SMEM, SMEM, VMEM, ANY, ANY], out_specs=(VMEM,) * 4,
            scratch_shapes=[whole, whole, table, scaled, acc, pltpu.SemaphoreType.DMA((2,))],
            name="plane_two",
        )(cols, x_cols, scales, a_tiles, x)
        y, kept2 = hold((y, kept2))
        q1, q2, q3, kept1 = pl.pallas_call(
            lambda *refs: first_kernel(*sizes, *refs),
            out_shape=(two, two, two, shape((2 * rows, half), f32)),
            in_specs=[SMEM, SMEM, SMEM, VMEM, ANY, ANY, ANY], out_specs=(VMEM,) * 4,
            scratch_shapes=[whole, whole, whole, table, scaled, acc, pltpu.SemaphoreType.DMA((3,))],
            name="plane_one",
        )(cols, x_cols, y_cols, scales, a_tiles, x, y)
        r1, r2, r3 = [move(p, slab_pairs(k)) for k, p in ((1, p1), (2, p2), (3, p3))]
        t1, t2, t3 = [move(q, slab_pairs(k, hubs)) for k, q in ((1, q1), (2, q2), (3, q3))]
        core = lax.axis_index("slab") % 2
        wide = lambda value: value.astype(f32)
        r1, r2, r3, mine = hold((r1, r2, r3, mine))
        theirs = move(mine, slab_pairs(1))
        same = kept2 + wide(r2)
        swapped = wide(r1) + wide(r3)
        own2 = jnp.where(core == 0, same, swapped)
        ahead2 = jnp.where(core == 0, swapped, same).astype(bf16)
        ahead2 = move(ahead2, ahead_pairs)
        column, lower = pl.pallas_call(
            lambda *refs: panel_kernel(tile, *refs),
            out_shape=(shape((rows, half), f32), shape((tile, tile), bf16)),
            in_specs=[SMEM] + [VMEM] * 4, out_specs=(VMEM, VMEM),
            scratch_shapes=[pltpu.VMEM((rows, tile), f32), pltpu.VMEM((tile, rows), f32), pltpu.VMEM((tile, rows), f32)],
            name="panel_step",
        )(panel, keep, got, mine, theirs)
        t1, t2, t3, lower = hold((t1, t2, t3, lower))
        lower = move(lower, slab_pairs(2))
        plane1 = kept1 + wide(t1) + wide(t2) + wide(t3)
        own1 = plane1[rows:]
        beside = move(plane1[:rows].astype(bf16), beside_pairs)
        ahead1 = move(own1.astype(bf16), even_ahead_pairs)
        out = pl.pallas_call(
            lambda *refs: final_kernel(tile, *refs),
            out_shape=shape((3, rows, half), f32),
            in_specs=[SMEM] + [VMEM] * 7, out_specs=VMEM, name="assemble",
        )(panel, column, lower, own2, own1, ahead2, ahead1, beside)
        return out.transpose(1, 0, 2)

    return body


def solution(mesh):
    return jax.shard_map(
        make_body(mesh.shape["blk"], mesh.shape["slab"]),
        mesh=mesh,
        in_specs=(P("blk", "slab"), P("blk", "slab", None), P("blk", "slab"), P("slab"), P()),
        out_specs=P("blk", None, "slab"),
        check_vma=False,
    )
```

```python
import jax
import jax.numpy as jnp
from jax import lax
from jax.experimental import pallas as pl
from jax.experimental.pallas import tpu as pltpu
from jax.sharding import PartitionSpec as P

ridge_shift = 0.05
AXES = ("blk", "slab")
HIGH = lax.Precision.HIGHEST
SMEM = pl.BlockSpec(memory_space=pltpu.SMEM)
ANY = pl.BlockSpec(memory_space=pl.ANY)
VMEM = pl.BlockSpec(memory_space=pltpu.VMEM)


def product(lhs, rhs, lhs_cols, rhs_cols, scaling, table, scaled, tile, slots, col_tiles, emit):
    for b in range(2):
        for c in range(col_tiles):
            table[b, c] = jnp.int32(slots)
    for b in range(2):
        for n in range(slots):
            col = rhs_cols[b, n]
            table[b, col] = jnp.int32(n)

    def left(t, carry):
        i = t // slots
        m = t % slots
        col = lhs_cols[i, m]
        live = col < col_tiles
        col = jnp.minimum(col, col_tiles - 1)
        other = [table[b, col] for b in range(2)]

        @pl.when(live & ((other[0] < slots) | (other[1] < slots)))
        def _():
            rows = pl.ds(pl.multiple_of(i * tile, tile), tile)
            cols = pl.ds(pl.multiple_of(m * tile, tile), tile)
            scaled[...] = (lhs[rows, cols].astype(jnp.float32) * scaling[pl.ds(col, 1), :]).astype(jnp.bfloat16)
            for b in range(2):

                @pl.when(other[b] < slots)
                def _():
                    cols = pl.ds(pl.multiple_of(other[b] * tile, tile), tile)
                    emit(i, b, lax.dot_general(
                        scaled[...], rhs[b * tile:(b + 1) * tile, cols],
                        (((1,), (1,)), ((), ())), preferred_element_type=jnp.float32))

        return carry

    lax.fori_loop(0, 2 * slots, left, 0)


def live_cols(tile_cols, tile_counts, cols, slots, col_tiles):
    for b in range(2):
        for n in range(slots):
            cols[b, n] = jnp.where(n < tile_counts[b], tile_cols[b, 0, n], col_tiles)


def pack_kernel(slots, col_tiles, tile_cols, tile_counts, a, out, held, cols, tail, sems):
    pieces = 4
    rows = a.shape[0]
    size = rows // pieces
    part = [pl.ds(p * size, size) for p in range(pieces)]
    reads = [pltpu.make_async_copy(a.at[part[p], :], held.at[part[p], :], sems.at[p]) for p in range(pieces)]
    writes = [pltpu.make_async_copy(held.at[part[p], :], out.at[part[p], :], sems.at[pieces + p]) for p in range(pieces)]
    for copy in reads:
        copy.start()
    live_cols(tile_cols, tile_counts, cols, slots, col_tiles)
    row = lax.broadcasted_iota(jnp.int32, tail.shape, 0)
    lane = lax.broadcasted_iota(jnp.int32, tail.shape, 1)
    value = jnp.zeros(tail.shape, jnp.float32)
    for b in range(2):
        for n in range(slots):
            value = jnp.where((row == b) & (lane == n), cols[b, n].astype(jnp.float32), value)
    tail[...] = value.astype(tail.dtype)
    last = pltpu.make_async_copy(
        tail, out.at[pl.ds(rows, tail.shape[0]), pl.ds(0, tail.shape[1])], sems.at[2 * pieces])
    last.start()
    for read, write in zip(reads, writes):
        read.wait()
        write.start()
    for write in writes:
        write.wait()
    last.wait()


def tail_cols(packed, rows, tails, ints, cols, sems, first):
    count = len(packed)
    lists = [pltpu.make_async_copy(
        packed[n].at[pl.ds(rows, tails.shape[1]), pl.ds(0, tails.shape[2])], tails.at[n], sems.at[first + n])
        for n in range(count)]
    for copy in lists:
        copy.start()

    def finish():
        scalars = [pltpu.make_async_copy(ints.at[n], cols[n], sems.at[first + count + n]) for n in range(count)]
        for n in range(count):
            lists[n].wait()
            ints[n] = tails[n].astype(jnp.float32)[:ints.shape[1]].astype(jnp.int32)
            scalars[n].start()
        for copy in scalars:
            copy.wait()

    return finish


def own_kernel(tile, slots, col_tiles, tile_cols, tile_counts, scaling, a, give, keep, cols, table, scaled, acc):
    slab = lax.axis_index("slab")
    core = slab % 2
    y_lo = slab // 2
    rows = acc.shape[1]
    acc[...] = jnp.zeros_like(acc)
    live_cols(tile_cols, tile_counts, cols, slots, col_tiles)

    def emit(i, b, value):
        acc[b, pl.ds(pl.multiple_of(i * tile, tile), tile), :] += value

    product(a, a, cols, cols, scaling, table, scaled, tile, slots, col_tiles, emit)
    give[:rows, :] = acc[y_lo]
    keep[:rows, :] = acc[y_lo]
    give[rows:, :] = acc[1 - y_lo, pl.ds(pl.multiple_of((1 - core) * tile, tile), tile), :]
    keep[rows:, :] = acc[1 - y_lo, pl.ds(pl.multiple_of(core * tile, tile), tile), :]


def fetch(copies, sems):
    started = [pltpu.make_async_copy(src, dst, sems.at[n]) for n, (src, dst) in enumerate(copies)]
    for copy in started:
        copy.start()
    return started


def adder(acc, tile):
    half = tile // 2

    def emit(i, b, value):
        at = pl.ds(pl.multiple_of(i * tile, tile), tile)
        acc[2 * b, at, :] += value[:, :half]
        acc[2 * b + 1, at, :] += value[:, half:]

    return emit


def second_kernel(tile, slots, col_tiles, tile_cols, tile_counts, scaling, a_any, x_any, p1, p2, p3, kept,
                  a, x, cols, x_cols, tail, ints, table, scaled, acc, sems):
    slab = lax.axis_index("slab")
    core = slab % 2
    rows = a.shape[0]
    finish = tail_cols([x_any], rows, tail, ints, [x_cols], sems, 2)
    copies = fetch([(a_any, a), (x_any.at[pl.ds(0, rows), :], x)], sems)
    args = (scaling, table, scaled, tile, slots, col_tiles, adder(acc, tile))
    finish()
    live_cols(tile_cols, tile_counts, cols, slots, col_tiles)
    acc[...] = jnp.zeros_like(acc)
    for copy in copies:
        copy.wait()

    @pl.when(core == 0)
    def _():
        product(a, x, cols, x_cols, *args)

    @pl.when(core == 1)
    def _():
        product(x, a, x_cols, cols, *args)

    kept[...] = acc[slab]
    for k, ref in ((1, p1), (2, p2), (3, p3)):
        ref[...] = acc[slab ^ k].astype(ref.dtype)


def first_kernel(tile, slots, col_tiles, tile_cols, tile_counts, scaling, a_any, x_any, y_any, q1, q2, q3, kept,
                 a, x, y, cols, x_cols, y_cols, tail, ints, table, scaled, acc, sems):
    slab = lax.axis_index("slab")
    core = slab % 2
    hub = (core + lax.axis_index("blk")) % 2 == 1
    rows = a.shape[0]

    def store(start):
        kept[start:start + rows, :] = acc[slab]
        for k, ref in ((1, q1), (2, q2), (3, q3)):
            ref[start:start + rows, :] = acc[slab ^ k].astype(ref.dtype)

    @pl.when(jnp.logical_not(hub))
    def _():
        kept[...] = jnp.zeros_like(kept)

    @pl.when(hub)
    def _():
        part = pl.ds(0, rows)
        finish = tail_cols([x_any, y_any], rows, tail, ints, [x_cols, y_cols], sems, 3)
        copies = fetch([(y_any.at[part, :], y), (x_any.at[part, :], x), (a_any, a)], sems)
        finish()
        live_cols(tile_cols, tile_counts, cols, slots, col_tiles)
        args = (scaling, table, scaled, tile, slots, col_tiles, adder(acc, tile))
        acc[...] = jnp.zeros_like(acc)
        for copy in copies:
            copy.wait()

        @pl.when(core == 0)
        def _():
            product(y, x, y_cols, x_cols, *args)

        @pl.when(core == 1)
        def _():
            product(y, a, y_cols, cols, *args)

        store(0)
        acc[...] = jnp.zeros_like(acc)

        @pl.when(core == 0)
        def _():
            product(a, y, cols, y_cols, *args)

        @pl.when(core == 1)
        def _():
            product(x, y, x_cols, y_cols, *args)

        store(rows)


def eliminate(matrix, size, group):
    tiles = size // 8
    v = matrix.reshape(tiles, 8, 128)
    ids = lax.broadcasted_iota(jnp.int32, (tiles, 8, 128), 0) * 8 + lax.broadcasted_iota(
        jnp.int32, (tiles, 8, 128), 1)
    pivots = [jnp.ones((8, 128), jnp.float32) for _ in range(tiles)]
    for j in range(0, size, group):
        s = {}
        for a in range(group):
            for b in range(a + 1):
                r = j + a
                s[a, b] = jnp.broadcast_to(v[r // 8, r % 8:r % 8 + 1, j + b:j + b + 1], (8, 128))
        rows = [jnp.broadcast_to(v[(j + a) // 8, (j + a) % 8:(j + a) % 8 + 1, :], (8, 128)) for a in range(group)]
        below = (j + group) // 8
        last = j + group >= size
        cols = [] if last else [
            jnp.broadcast_to(v[below:, :, j + b:j + b + 1], (tiles - below, 8, 128)) for b in range(group)]
        low = {}
        inverse = []
        for b in range(group):
            inverse.append(1.0 / s[b, b])
            for a in range(b + 1, group):
                low[a, b] = s[a, b] * inverse[b]
            for a in range(b + 1, group):
                for c in range(b + 1, a + 1):
                    s[a, c] = s[a, c] - low[a, b] * s[c, b]
        for a in range(group):
            for b in range(a):
                rows[a] = rows[a] - low[a, b] * rows[b]
        top = j // 8
        kept = v[top]
        for a in range(group):
            here = ids[top] == j + a
            kept = jnp.where(here, rows[a], kept)
            pivots[top] = jnp.where(here, s[a, a], pivots[top])
        pieces = [v[:top]] if top else []
        pieces.append(kept[None])
        if not last:
            steps = []
            update = None
            for b in range(group):
                step = cols[b]
                for k in range(b):
                    step = step - steps[k] * s[b, k][None]
                steps.append(step * inverse[b][None])
                term = steps[b] * rows[b][None]
                update = term if update is None else update + term
            pieces.append(v[below:] - update)
        v = jnp.concatenate(pieces, 0) if len(pieces) > 1 else pieces[0]
    return (v * lax.rsqrt(jnp.stack(pivots))).reshape(size, 128)


def panel_factor(w, u, first, stop, size, group):
    n, width = w.shape
    for start in range(first, stop, size):
        base = start // 128 * 128
        square = w[start:start + size, base:base + 128]
        if start > base:
            square = pltpu.roll(square, 128 - (start - base), 1)
        lane = lax.broadcasted_iota(jnp.int32, (size, 128), 1)
        row = lax.broadcasted_iota(jnp.int32, (size, 128), 0)
        square = jnp.where(lane < size, square, jnp.where(lane - size == row, 1.0, 0.0))
        inverse = eliminate(square, size, group)[:, size:2 * size]
        strip = lax.dot_general(
            inverse, w[start:start + size, :], (((1,), (0,)), ((), ())),
            precision=HIGH, preferred_element_type=jnp.float32)
        lane = lax.broadcasted_iota(jnp.int32, (size, width), 1)
        row = lax.broadcasted_iota(jnp.int32, (size, width), 0)
        strip = jnp.where(lane - start >= row, strip, 0.0)
        u[start:start + size, :] = strip
        if start + size < n:
            w[start + size:, :] = w[start + size:, :] - lax.dot_general(
                strip[:, start + size:n], strip, (((0,), (0,)), ((), ())),
                precision=HIGH, preferred_element_type=jnp.float32)


def holds_panel(panel):
    block = panel[0]
    pos = block % 2
    return (block // 2 == lax.axis_index("blk")) & (pos == lax.axis_index("slab") // 2), pos


def panel_head(tile, panel, keep, got, mine, theirs, column, top, rest, total, w, u, sems):
    slab = lax.axis_index("slab")
    core = slab % 2
    y_lo = slab // 2
    half = tile // 2
    holds, pos = holds_panel(panel)
    rows = total.shape[0]
    total[...] = keep[:rows, :] + got[:rows, :]
    total[pl.ds(pl.multiple_of(core * tile, tile), tile), :] += mine[...]
    total[pl.ds(pl.multiple_of((1 - core) * tile, tile), tile), :] += theirs[...]
    eye = jnp.where(
        lax.broadcasted_iota(jnp.int32, (tile, tile), 0) == lax.broadcasted_iota(jnp.int32, (tile, tile), 1),
        jnp.float32(ridge_shift), jnp.float32(0.0))
    total[pl.ds(pl.multiple_of(y_lo * tile, tile), tile), :] += eye

    @pl.when(core == 0)
    def _():
        column[...] = total[:, :half]

    @pl.when(core == 1)
    def _():
        column[...] = total[:, half:]

    @pl.when(holds)
    def _():
        square = total[pl.ds(pl.multiple_of(pos * tile, tile), tile), :]
        w[:, :tile] = (square + square.T) * 0.5
        w[:, tile:] = total[pl.ds(pl.multiple_of((1 - pos) * tile, tile), tile), :].T
        panel_factor(w, u, 0, half, 64, 8)
        for copy in fetch([(u.at[pl.ds(0, half), :], top), (w.at[pl.ds(half, half), :], rest)], sems):
            copy.wait()


def panel_tail(tile, panel, top, rest, before, column, lower, w, u, low, mine, sems):
    core = lax.axis_index("slab") % 2
    half = tile // 2
    holds, pos = holds_panel(panel)

    @pl.when(holds)
    def _():
        for copy in fetch([(top, u.at[pl.ds(0, half), :]), (rest, w.at[pl.ds(half, half), :])], sems):
            copy.wait()
        panel_factor(w, u, half, tile, 64, 8)
        low[...] = u[:, tile:].astype(low.dtype)
        out = pltpu.make_async_copy(low, lower, sems.at[0])
        out.start()
        rows = pl.ds(pl.multiple_of(core * half, half), half)
        mine[pl.ds(pl.multiple_of(pos * tile, tile), tile), :] = u[rows, :tile].T
        mine[pl.ds(pl.multiple_of((1 - pos) * tile, tile), tile), :] = u[rows, tile:].T
        back = pltpu.make_async_copy(mine, column, sems.at[1])
        back.start()
        out.wait()
        back.wait()


def final_kernel(tile, column, own2, plane1, ahead2, ahead1, beside, out):
    group = lax.axis_index("blk")
    rows = column.shape[0]
    out[0] = column[...]
    out[2] = own2[...] + ahead2[...].astype(jnp.float32)
    late = jnp.where(group % 2 == 1, plane1[rows:, :], ahead1[...].astype(jnp.float32))
    out[1] = late + beside[...].astype(jnp.float32)


def reduce_kernel(tile, panel, lower_any, band, out, lower, corner, sems):
    slab = lax.axis_index("slab")
    core = slab % 2
    y_lo = slab // 2
    half = tile // 2
    block = panel[0]

    @pl.when((block // 2 == lax.axis_index("blk")) & (block % 2 != y_lo))
    def _():
        here = out.at[0, pl.ds(pl.multiple_of(y_lo * tile, tile), tile), :]
        for copy in fetch([(lower_any, lower), (here, corner)], sems):
            copy.wait()
        left = lower[...].astype(jnp.float32)
        right = jnp.where(core == 0, left[:, :half], left[:, half:])
        corner[...] = corner[...] - lax.dot_general(
            left, right, (((0,), (0,)), ((), ())), precision=HIGH, preferred_element_type=jnp.float32)
        back = pltpu.make_async_copy(corner, here, sems.at[2])
        back.start()
        back.wait()


def make_body(groups, slabs):
    devices = [(g, s) for g in range(groups) for s in range(slabs)]
    at = lambda g, s: (g % groups) * slabs + s
    forward = lambda s: s % 2 == 0
    hubs = [(g, s) for g, s in devices if (g + s) % 2 == 1]
    far_pairs = [(at(g, s), at(g + (2 if forward(s) else -2), s)) for g, s in devices]
    near_pairs = [(at(g + (-1 if forward(s) else 1), s), at(g, s)) for g, s in hubs]
    slab_pairs = lambda k, among=devices: [(at(g, s), at(g, s ^ k)) for g, s in among]
    ahead_pairs = [(at(g, s), at(g + 2, s)) for g, s in devices]
    even_ahead_pairs = [(at(g, s), at(g + 2, s)) for g, s in devices if g % 2 == 0]
    beside_pairs = [(at(g, s), at(g ^ 1, s)) for g, s in devices]

    hold = lax.optimization_barrier

    def move(value, pairs):
        return lax.ppermute(value, AXES, pairs)

    def body(a_tiles, tile_cols, tile_counts, scaling, panel):
        rows = a_tiles.shape[0]
        blocks = tile_cols.shape[0]
        slots = tile_cols.shape[2]
        tile = rows // blocks
        col_tiles = scaling.shape[0] // tile
        half = tile // 2
        f32 = jnp.float32
        bf16 = jnp.bfloat16
        shape = jax.ShapeDtypeStruct
        scales = scaling.reshape(col_tiles, tile)
        cols = pltpu.SMEM((2, slots), jnp.int32)
        tail = pltpu.VMEM((16, 128), bf16)
        counts = tile_counts[:, 0]
        moved = pltpu.SMEM((8, 128), jnp.int32)
        dma = lambda n: pltpu.SemaphoreType.DMA((n,))
        packed = pl.pallas_call(
            lambda *refs: pack_kernel(slots, col_tiles, *refs),
            out_shape=shape((rows + 16, a_tiles.shape[1]), bf16),
            in_specs=[SMEM, SMEM, ANY], out_specs=ANY, scratch_shapes=[pltpu.VMEM(a_tiles.shape, bf16), cols, tail, dma(9)], name="pack",
        )(tile_cols, counts, a_tiles)
        table = pltpu.SMEM((2, col_tiles + 1), jnp.int32)
        scaled = pltpu.VMEM((tile, tile), bf16)
        sizes = (tile, slots, col_tiles)
        own_tiles, packed = hold((a_tiles, packed))
        x = move(packed, far_pairs)
        y = move(packed, near_pairs)
        give, keep = pl.pallas_call(
            lambda *refs: own_kernel(*sizes, *refs),
            out_shape=(shape((rows + tile, tile), f32), shape((rows + tile, tile), f32)),
            in_specs=[SMEM, SMEM, VMEM, VMEM], out_specs=(VMEM, VMEM),
            scratch_shapes=[cols, table, scaled, pltpu.VMEM((2, rows, tile), f32)], name="plane_zero",
            compiler_params=pltpu.CompilerParams(vmem_limit_bytes=64 * 2**20 - 2**16),
        )(tile_cols, counts, scales, own_tiles)
        got = move(give, slab_pairs(1))
        mine = move(keep[rows:] + got[rows:], slab_pairs(2))
        part = shape((rows, half), bf16)
        two = shape((2 * rows, half), bf16)
        whole = pltpu.VMEM(a_tiles.shape, bf16)
        acc = pltpu.VMEM((4, rows, half), f32)
        p1, p2, p3, kept2 = pl.pallas_call(
            lambda *refs: second_kernel(*sizes, *refs),
            out_shape=(part, part, part, shape((rows, half), f32)),
            in_specs=[SMEM, SMEM, VMEM, ANY, ANY], out_specs=(VMEM,) * 4,
            scratch_shapes=[whole, whole, cols, moved, pltpu.VMEM((1, 16, 128), bf16), pltpu.VMEM((1, 8, 128), jnp.int32), table, scaled, acc, dma(4)],
            name="plane_two",
        )(tile_cols, counts, scales, a_tiles, x)
        y, kept2 = hold((y, kept2))
        q1, q2, q3, kept1 = pl.pallas_call(
            lambda *refs: first_kernel(*sizes, *refs),
            out_shape=(two, two, two, shape((2 * rows, half), f32)),
            in_specs=[SMEM, SMEM, VMEM, ANY, ANY, ANY], out_specs=(VMEM,) * 4,
            scratch_shapes=[whole, whole, whole, cols, moved, moved, pltpu.VMEM((2, 16, 128), bf16), pltpu.VMEM((2, 8, 128), jnp.int32), table, scaled, acc, dma(7)],
            name="plane_one",
        )(tile_cols, counts, scales, a_tiles, x, y)
        r1, r2, r3 = [move(p, slab_pairs(k)) for k, p in ((1, p1), (2, p2), (3, p3))]
        t1, t2, t3 = [move(q, slab_pairs(k, hubs)) for k, q in ((1, q1), (2, q2), (3, q3))]
        core = lax.axis_index("slab") % 2
        wide = lambda value: value.astype(f32)
        r1, r2, r3, mine = hold((r1, r2, r3, mine))
        theirs = move(mine, slab_pairs(1))
        same = kept2 + wide(r2)
        swapped = wide(r1) + wide(r3)
        own2 = jnp.where(core == 0, same, swapped)
        ahead2 = jnp.where(core == 0, swapped, same).astype(bf16)
        ahead2 = move(ahead2, ahead_pairs)
        column, top, rest = pl.pallas_call(
            lambda *refs: panel_head(tile, *refs),
            out_shape=(shape((rows, half), f32), shape((half, rows), f32), shape((half, rows), f32)),
            in_specs=[SMEM] + [VMEM] * 4, out_specs=(VMEM, ANY, ANY),
            scratch_shapes=[pltpu.VMEM((rows, tile), f32), pltpu.VMEM((tile, rows), f32), pltpu.VMEM((tile, rows), f32),
                            dma(2)],
            name="panel_head",
        )(panel, keep, got, mine, theirs)
        t1, t2, t3, column = hold((t1, t2, t3, column))
        plane1 = kept1 + wide(t1) + wide(t2) + wide(t3)
        beside, ahead1, top = hold((plane1[:rows].astype(bf16), plane1[rows:].astype(bf16), top))
        beside = move(beside, beside_pairs)
        ahead1 = move(ahead1, even_ahead_pairs)
        column, lower = pl.pallas_call(
            lambda *refs: panel_tail(tile, *refs),
            out_shape=(shape((rows, half), f32), shape((tile, tile), bf16)),
            in_specs=[SMEM, ANY, ANY, ANY], out_specs=(ANY, ANY), input_output_aliases={3: 0},
            scratch_shapes=[pltpu.VMEM((tile, rows), f32), pltpu.VMEM((tile, rows), f32), pltpu.VMEM((tile, tile), bf16),
                            pltpu.VMEM((rows, half), f32), dma(2)],
            name="panel_tail",
            compiler_params=pltpu.CompilerParams(vmem_limit_bytes=64 * 2**20 - 2**16),
        )(panel, top, rest, column)
        lower = move(lower, slab_pairs(2))
        out = pl.pallas_call(
            lambda *refs: final_kernel(tile, *refs),
            out_shape=shape((3, rows, half), f32),
            in_specs=[VMEM] * 6, out_specs=VMEM, name="assemble",
            compiler_params=pltpu.CompilerParams(vmem_limit_bytes=64 * 2**20 - 2**16),
        )(column, own2, plane1, ahead2, ahead1, beside)
        out = pl.pallas_call(
            lambda *refs: reduce_kernel(tile, *refs),
            out_shape=shape((3, rows, half), f32),
            in_specs=[SMEM, ANY, ANY], out_specs=ANY, input_output_aliases={2: 0},
            scratch_shapes=[pltpu.VMEM((tile, tile), bf16), pltpu.VMEM((tile, half), f32), dma(3)], name="reduce",
        )(panel, lower, out)
        return out.transpose(1, 0, 2)

    return body


def solution(mesh):
    return jax.shard_map(
        make_body(mesh.shape["blk"], mesh.shape["slab"]),
        mesh=mesh,
        in_specs=(P("blk", "slab"), P("blk", "slab", None), P("blk", "slab"), P("slab"), P()),
        out_specs=P("blk", None, "slab"),
        check_vma=False,
    )
```

```python
import jax
import jax.numpy as jnp
from jax import lax
from jax.experimental import pallas as pl
from jax.experimental.pallas import tpu as pltpu
from jax.sharding import PartitionSpec as P

ridge_shift = 0.05
AXES = ("blk", "slab")
HIGH = lax.Precision.HIGHEST
SMEM = pl.BlockSpec(memory_space=pltpu.SMEM)
ANY = pl.BlockSpec(memory_space=pl.ANY)
VMEM = pl.BlockSpec(memory_space=pltpu.VMEM)


def product(lhs, rhs, lhs_cols, rhs_cols, scaling, table, scaled, tile, slots, col_tiles, emit):
    for b in range(2):
        for c in range(col_tiles):
            table[b, c] = jnp.int32(slots)
    for b in range(2):
        for n in range(slots):
            col = rhs_cols[b, n]
            table[b, col] = jnp.int32(n)

    def left(t, carry):
        i = t // slots
        m = t % slots
        col = lhs_cols[i, m]
        live = col < col_tiles
        col = jnp.minimum(col, col_tiles - 1)
        other = [table[b, col] for b in range(2)]

        @pl.when(live & ((other[0] < slots) | (other[1] < slots)))
        def _():
            rows = pl.ds(pl.multiple_of(i * tile, tile), tile)
            cols = pl.ds(pl.multiple_of(m * tile, tile), tile)
            scaled[...] = (lhs[rows, cols].astype(jnp.float32) * scaling[pl.ds(col, 1), :]).astype(jnp.bfloat16)
            for b in range(2):

                @pl.when(other[b] < slots)
                def _():
                    cols = pl.ds(pl.multiple_of(other[b] * tile, tile), tile)
                    emit(i, b, lax.dot_general(
                        scaled[...], rhs[b * tile:(b + 1) * tile, cols],
                        (((1,), (1,)), ((), ())), preferred_element_type=jnp.float32))

        return carry

    lax.fori_loop(0, 2 * slots, left, 0)


def live_cols(tile_cols, tile_counts, cols, slots, col_tiles):
    for b in range(2):
        for n in range(slots):
            cols[b, n] = jnp.where(n < tile_counts[b], tile_cols[b, 0, n], col_tiles)


def pack_kernel(slots, col_tiles, tile_cols, tile_counts, a, out, held, cols, tail, sems):
    pieces = 4
    rows = a.shape[0]
    size = rows // pieces
    part = [pl.ds(p * size, size) for p in range(pieces)]
    reads = [pltpu.make_async_copy(a.at[part[p], :], held.at[part[p], :], sems.at[p]) for p in range(pieces)]
    writes = [pltpu.make_async_copy(held.at[part[p], :], out.at[part[p], :], sems.at[pieces + p]) for p in range(pieces)]
    for copy in reads:
        copy.start()
    live_cols(tile_cols, tile_counts, cols, slots, col_tiles)
    row = lax.broadcasted_iota(jnp.int32, tail.shape, 0)
    lane = lax.broadcasted_iota(jnp.int32, tail.shape, 1)
    value = jnp.zeros(tail.shape, jnp.float32)
    for b in range(2):
        for n in range(slots):
            value = jnp.where((row == b) & (lane == n), cols[b, n].astype(jnp.float32), value)
    tail[...] = value.astype(tail.dtype)
    last = pltpu.make_async_copy(
        tail, out.at[pl.ds(rows, tail.shape[0]), pl.ds(0, tail.shape[1])], sems.at[2 * pieces])
    last.start()
    for read, write in zip(reads, writes):
        read.wait()
        write.start()
    for write in writes:
        write.wait()
    last.wait()


def tail_cols(packed, rows, tails, ints, cols, sems, first):
    count = len(packed)
    lists = [pltpu.make_async_copy(
        packed[n].at[pl.ds(rows, tails.shape[1]), pl.ds(0, tails.shape[2])], tails.at[n], sems.at[first + n])
        for n in range(count)]
    for copy in lists:
        copy.start()

    def finish():
        scalars = [pltpu.make_async_copy(ints.at[n], cols[n], sems.at[first + count + n]) for n in range(count)]
        for n in range(count):
            lists[n].wait()
            ints[n] = tails[n].astype(jnp.float32)[:ints.shape[1]].astype(jnp.int32)
            scalars[n].start()
        for copy in scalars:
            copy.wait()

    return finish


def own_kernel(tile, slots, col_tiles, tile_cols, tile_counts, scaling, a, give, keep, cols, table, scaled, acc):
    slab = lax.axis_index("slab")
    core = slab % 2
    y_lo = slab // 2
    rows = acc.shape[1]
    acc[...] = jnp.zeros_like(acc)
    live_cols(tile_cols, tile_counts, cols, slots, col_tiles)

    def emit(i, b, value):
        acc[b, pl.ds(pl.multiple_of(i * tile, tile), tile), :] += value

    product(a, a, cols, cols, scaling, table, scaled, tile, slots, col_tiles, emit)
    give[:rows, :] = acc[y_lo]
    keep[:rows, :] = acc[y_lo]
    give[rows:, :] = acc[1 - y_lo, pl.ds(pl.multiple_of((1 - core) * tile, tile), tile), :]
    keep[rows:, :] = acc[1 - y_lo, pl.ds(pl.multiple_of(core * tile, tile), tile), :]


def fetch(copies, sems):
    started = [pltpu.make_async_copy(src, dst, sems.at[n]) for n, (src, dst) in enumerate(copies)]
    for copy in started:
        copy.start()
    return started


def adder(acc, tile):
    half = tile // 2

    def emit(i, b, value):
        at = pl.ds(pl.multiple_of(i * tile, tile), tile)
        acc[2 * b, at, :] += value[:, :half]
        acc[2 * b + 1, at, :] += value[:, half:]

    return emit


def second_kernel(tile, slots, col_tiles, tile_cols, tile_counts, scaling, a_any, x_any, p1, p2, p3, kept,
                  a, x, cols, x_cols, tail, ints, table, scaled, acc, sems):
    slab = lax.axis_index("slab")
    core = slab % 2
    rows = a.shape[0]
    finish = tail_cols([x_any], rows, tail, ints, [x_cols], sems, 2)
    copies = fetch([(a_any, a), (x_any.at[pl.ds(0, rows), :], x)], sems)
    args = (scaling, table, scaled, tile, slots, col_tiles, adder(acc, tile))
    finish()
    live_cols(tile_cols, tile_counts, cols, slots, col_tiles)
    acc[...] = jnp.zeros_like(acc)
    for copy in copies:
        copy.wait()

    @pl.when(core == 0)
    def _():
        product(a, x, cols, x_cols, *args)

    @pl.when(core == 1)
    def _():
        product(x, a, x_cols, cols, *args)

    kept[...] = acc[slab]
    for k, ref in ((1, p1), (2, p2), (3, p3)):
        ref[...] = acc[slab ^ k].astype(ref.dtype)


def first_kernel(tile, slots, col_tiles, tile_cols, tile_counts, scaling, a_any, x_any, y_any, q1, q2, q3, kept,
                 a, x, y, cols, x_cols, y_cols, tail, ints, table, scaled, acc, sems):
    slab = lax.axis_index("slab")
    core = slab % 2
    hub = (core + lax.axis_index("blk")) % 2 == 1
    rows = a.shape[0]

    def store(start):
        kept[start:start + rows, :] = acc[slab]
        for k, ref in ((1, q1), (2, q2), (3, q3)):
            ref[start:start + rows, :] = acc[slab ^ k].astype(ref.dtype)

    @pl.when(jnp.logical_not(hub))
    def _():
        kept[...] = jnp.zeros_like(kept)

    @pl.when(hub)
    def _():
        part = pl.ds(0, rows)
        finish = tail_cols([x_any, y_any], rows, tail, ints, [x_cols, y_cols], sems, 3)
        y_copy = pltpu.make_async_copy(y_any.at[part, :], y, sems.at[0])
        x_copy = pltpu.make_async_copy(x_any.at[part, :], x, sems.at[1])
        a_copy = pltpu.make_async_copy(a_any, a, sems.at[2])
        y_copy.start()

        @pl.when(core == 0)
        def _():
            x_copy.start()
            a_copy.start()

        @pl.when(core == 1)
        def _():
            a_copy.start()
            x_copy.start()

        finish()
        live_cols(tile_cols, tile_counts, cols, slots, col_tiles)
        args = (scaling, table, scaled, tile, slots, col_tiles, adder(acc, tile))
        acc[...] = jnp.zeros_like(acc)
        y_copy.wait()

        @pl.when(core == 0)
        def _():
            x_copy.wait()
            product(y, x, y_cols, x_cols, *args)

        @pl.when(core == 1)
        def _():
            a_copy.wait()
            product(y, a, y_cols, cols, *args)

        store(0)
        acc[...] = jnp.zeros_like(acc)

        @pl.when(core == 0)
        def _():
            a_copy.wait()
            product(a, y, cols, y_cols, *args)

        @pl.when(core == 1)
        def _():
            x_copy.wait()
            product(x, y, x_cols, y_cols, *args)

        store(rows)


def eliminate(matrix, size, group):
    tiles = size // 8
    v = matrix.reshape(tiles, 8, 128)
    ids = lax.broadcasted_iota(jnp.int32, (tiles, 8, 128), 0) * 8 + lax.broadcasted_iota(
        jnp.int32, (tiles, 8, 128), 1)
    pivots = [jnp.ones((8, 128), jnp.float32) for _ in range(tiles)]
    for j in range(0, size, group):
        s = {}
        for a in range(group):
            for b in range(a + 1):
                r = j + a
                s[a, b] = jnp.broadcast_to(v[r // 8, r % 8:r % 8 + 1, j + b:j + b + 1], (8, 128))
        rows = [jnp.broadcast_to(v[(j + a) // 8, (j + a) % 8:(j + a) % 8 + 1, :], (8, 128)) for a in range(group)]
        below = (j + group) // 8
        last = j + group >= size
        cols = [] if last else [
            jnp.broadcast_to(v[below:, :, j + b:j + b + 1], (tiles - below, 8, 128)) for b in range(group)]
        low = {}
        inverse = []
        for b in range(group):
            inverse.append(1.0 / s[b, b])
            for a in range(b + 1, group):
                low[a, b] = s[a, b] * inverse[b]
            for a in range(b + 1, group):
                for c in range(b + 1, a + 1):
                    s[a, c] = s[a, c] - low[a, b] * s[c, b]
        for a in range(group):
            for b in range(a):
                rows[a] = rows[a] - low[a, b] * rows[b]
        top = j // 8
        kept = v[top]
        for a in range(group):
            here = ids[top] == j + a
            kept = jnp.where(here, rows[a], kept)
            pivots[top] = jnp.where(here, s[a, a], pivots[top])
        pieces = [v[:top]] if top else []
        pieces.append(kept[None])
        if not last:
            steps = []
            update = None
            for b in range(group):
                step = cols[b]
                for k in range(b):
                    step = step - steps[k] * s[b, k][None]
                steps.append(step * inverse[b][None])
                term = steps[b] * rows[b][None]
                update = term if update is None else update + term
            pieces.append(v[below:] - update)
        v = jnp.concatenate(pieces, 0) if len(pieces) > 1 else pieces[0]
    return (v * lax.rsqrt(jnp.stack(pivots))).reshape(size, 128)


def panel_factor(w, u, first, stop, size, group):
    n, width = w.shape
    for start in range(first, stop, size):
        base = start // 128 * 128
        square = w[start:start + size, base:base + 128]
        if start > base:
            square = pltpu.roll(square, 128 - (start - base), 1)
        lane = lax.broadcasted_iota(jnp.int32, (size, 128), 1)
        row = lax.broadcasted_iota(jnp.int32, (size, 128), 0)
        square = jnp.where(lane < size, square, jnp.where(lane - size == row, 1.0, 0.0))
        inverse = eliminate(square, size, group)[:, size:2 * size]
        strip = lax.dot_general(
            inverse, w[start:start + size, :], (((1,), (0,)), ((), ())),
            precision=HIGH, preferred_element_type=jnp.float32)
        lane = lax.broadcasted_iota(jnp.int32, (size, width), 1)
        row = lax.broadcasted_iota(jnp.int32, (size, width), 0)
        strip = jnp.where(lane - start >= row, strip, 0.0)
        u[start:start + size, :] = strip
        if start + size < n:
            w[start + size:, :] = w[start + size:, :] - lax.dot_general(
                strip[:, start + size:n], strip, (((0,), (0,)), ((), ())),
                precision=HIGH, preferred_element_type=jnp.float32)


def holds_panel(panel):
    block = panel[0]
    pos = block % 2
    return (block // 2 == lax.axis_index("blk")) & (pos == lax.axis_index("slab") // 2), pos


def panel_head(tile, panel, keep, got, mine, theirs, column, top, rest, total, w, u, sems):
    slab = lax.axis_index("slab")
    core = slab % 2
    y_lo = slab // 2
    half = tile // 2
    holds, pos = holds_panel(panel)
    rows = total.shape[0]
    total[...] = keep[:rows, :] + got[:rows, :]
    total[pl.ds(pl.multiple_of(core * tile, tile), tile), :] += mine[...]
    total[pl.ds(pl.multiple_of((1 - core) * tile, tile), tile), :] += theirs[...]
    eye = jnp.where(
        lax.broadcasted_iota(jnp.int32, (tile, tile), 0) == lax.broadcasted_iota(jnp.int32, (tile, tile), 1),
        jnp.float32(ridge_shift), jnp.float32(0.0))
    total[pl.ds(pl.multiple_of(y_lo * tile, tile), tile), :] += eye

    @pl.when(core == 0)
    def _():
        column[...] = total[:, :half]

    @pl.when(core == 1)
    def _():
        column[...] = total[:, half:]

    @pl.when(holds)
    def _():
        square = total[pl.ds(pl.multiple_of(pos * tile, tile), tile), :]
        w[:, :tile] = (square + square.T) * 0.5
        w[:, tile:] = total[pl.ds(pl.multiple_of((1 - pos) * tile, tile), tile), :].T
        panel_factor(w, u, 0, half, 64, 8)
        for copy in fetch([(u.at[pl.ds(0, half), :], top), (w.at[pl.ds(half, half), :], rest)], sems):
            copy.wait()


def panel_tail(tile, panel, top, rest, before, column, lower, w, u, low, mine, sems):
    core = lax.axis_index("slab") % 2
    half = tile // 2
    holds, pos = holds_panel(panel)

    @pl.when(holds)
    def _():
        for copy in fetch([(top, u.at[pl.ds(0, half), :]), (rest, w.at[pl.ds(half, half), :])], sems):
            copy.wait()
        panel_factor(w, u, half, tile, 64, 8)
        low[...] = u[:, tile:].astype(low.dtype)
        out = pltpu.make_async_copy(low, lower, sems.at[0])
        out.start()
        rows = pl.ds(pl.multiple_of(core * half, half), half)
        mine[pl.ds(pl.multiple_of(pos * tile, tile), tile), :] = u[rows, :tile].T
        mine[pl.ds(pl.multiple_of((1 - pos) * tile, tile), tile), :] = u[rows, tile:].T
        back = pltpu.make_async_copy(mine, column, sems.at[1])
        back.start()
        out.wait()
        back.wait()


def final_kernel(tile, column, own2, own1, ahead2, ahead1, beside, out):
    group = lax.axis_index("blk")
    rows = column.shape[0]
    out[0] = column[...]
    out[2] = own2[...] + ahead2[...].astype(jnp.float32)
    late = jnp.where(group % 2 == 1, own1[...], ahead1[...].astype(jnp.float32))
    out[1] = late + beside[...].astype(jnp.float32)


def reduce_kernel(tile, panel, lower_any, band, out, lower, corner, sems):
    slab = lax.axis_index("slab")
    core = slab % 2
    y_lo = slab // 2
    half = tile // 2
    block = panel[0]

    @pl.when((block // 2 == lax.axis_index("blk")) & (block % 2 != y_lo))
    def _():
        here = out.at[0, pl.ds(pl.multiple_of(y_lo * tile, tile), tile), :]
        for copy in fetch([(lower_any, lower), (here, corner)], sems):
            copy.wait()
        left = lower[...].astype(jnp.float32)
        right = jnp.where(core == 0, left[:, :half], left[:, half:])
        corner[...] = corner[...] - lax.dot_general(
            left, right, (((0,), (0,)), ((), ())), precision=HIGH, preferred_element_type=jnp.float32)
        back = pltpu.make_async_copy(corner, here, sems.at[2])
        back.start()
        back.wait()


def make_body(groups, slabs):
    devices = [(g, s) for g in range(groups) for s in range(slabs)]
    at = lambda g, s: (g % groups) * slabs + s
    forward = lambda s: s % 2 == 0
    hubs = [(g, s) for g, s in devices if (g + s) % 2 == 1]
    far_pairs = [(at(g, s), at(g + (2 if forward(s) else -2), s)) for g, s in devices]
    near_pairs = [(at(g + (-1 if forward(s) else 1), s), at(g, s)) for g, s in hubs]
    slab_pairs = lambda k, among=devices: [(at(g, s), at(g, s ^ k)) for g, s in among]
    ahead_pairs = [(at(g, s), at(g + 2, s)) for g, s in devices]
    even_ahead_pairs = [(at(g, s), at(g + 2, s)) for g, s in devices if g % 2 == 0]
    beside_pairs = [(at(g, s), at(g ^ 1, s)) for g, s in devices]

    hold = lax.optimization_barrier

    def move(value, pairs):
        return lax.ppermute(value, AXES, pairs)

    def body(a_tiles, tile_cols, tile_counts, scaling, panel):
        rows = a_tiles.shape[0]
        blocks = tile_cols.shape[0]
        slots = tile_cols.shape[2]
        tile = rows // blocks
        col_tiles = scaling.shape[0] // tile
        half = tile // 2
        f32 = jnp.float32
        bf16 = jnp.bfloat16
        shape = jax.ShapeDtypeStruct
        scales = scaling.reshape(col_tiles, tile)
        cols = pltpu.SMEM((2, slots), jnp.int32)
        tail = pltpu.VMEM((16, 128), bf16)
        counts = tile_counts[:, 0]
        moved = pltpu.SMEM((8, 128), jnp.int32)
        dma = lambda n: pltpu.SemaphoreType.DMA((n,))
        packed = pl.pallas_call(
            lambda *refs: pack_kernel(slots, col_tiles, *refs),
            out_shape=shape((rows + 16, a_tiles.shape[1]), bf16),
            in_specs=[SMEM, SMEM, ANY], out_specs=ANY, scratch_shapes=[pltpu.VMEM(a_tiles.shape, bf16), cols, tail, dma(9)], name="pack",
        )(tile_cols, counts, a_tiles)
        table = pltpu.SMEM((2, col_tiles + 1), jnp.int32)
        scaled = pltpu.VMEM((tile, tile), bf16)
        sizes = (tile, slots, col_tiles)
        own_tiles, packed = hold((a_tiles, packed))
        x = move(packed, far_pairs)
        y = move(packed, near_pairs)
        give, keep = pl.pallas_call(
            lambda *refs: own_kernel(*sizes, *refs),
            out_shape=(shape((rows + tile, tile), f32), shape((rows + tile, tile), f32)),
            in_specs=[SMEM, SMEM, VMEM, VMEM], out_specs=(VMEM, VMEM),
            scratch_shapes=[cols, table, scaled, pltpu.VMEM((2, rows, tile), f32)], name="plane_zero",
            compiler_params=pltpu.CompilerParams(vmem_limit_bytes=64 * 2**20 - 2**16),
        )(tile_cols, counts, scales, own_tiles)
        got = move(give, slab_pairs(1))
        mine = move(keep[rows:] + got[rows:], slab_pairs(2))
        part = shape((rows, half), bf16)
        two = shape((2 * rows, half), bf16)
        whole = pltpu.VMEM(a_tiles.shape, bf16)
        acc = pltpu.VMEM((4, rows, half), f32)
        p1, p2, p3, kept2 = pl.pallas_call(
            lambda *refs: second_kernel(*sizes, *refs),
            out_shape=(part, part, part, shape((rows, half), f32)),
            in_specs=[SMEM, SMEM, VMEM, ANY, ANY], out_specs=(VMEM,) * 4,
            scratch_shapes=[whole, whole, cols, moved, pltpu.VMEM((1, 16, 128), bf16), pltpu.VMEM((1, 8, 128), jnp.int32), table, scaled, acc, dma(4)],
            name="plane_two",
        )(tile_cols, counts, scales, a_tiles, x)
        y, kept2 = hold((y, kept2))
        q1, q2, q3, kept1 = pl.pallas_call(
            lambda *refs: first_kernel(*sizes, *refs),
            out_shape=(two, two, two, shape((2 * rows, half), f32)),
            in_specs=[SMEM, SMEM, VMEM, ANY, ANY, ANY], out_specs=(VMEM,) * 4,
            scratch_shapes=[whole, whole, whole, cols, moved, moved, pltpu.VMEM((2, 16, 128), bf16), pltpu.VMEM((2, 8, 128), jnp.int32), table, scaled, acc, dma(7)],
            name="plane_one",
        )(tile_cols, counts, scales, a_tiles, x, y)
        r1, r2, r3 = [move(p, slab_pairs(k)) for k, p in ((1, p1), (2, p2), (3, p3))]
        t1, t2, t3 = [move(q, slab_pairs(k, hubs)) for k, q in ((1, q1), (2, q2), (3, q3))]
        core = lax.axis_index("slab") % 2
        wide = lambda value: value.astype(f32)
        r1, r2, r3, mine = hold((r1, r2, r3, mine))
        theirs = move(mine, slab_pairs(1))
        same = kept2 + wide(r2)
        swapped = wide(r1) + wide(r3)
        own2 = jnp.where(core == 0, same, swapped)
        ahead2 = jnp.where(core == 0, swapped, same).astype(bf16)
        ahead2 = move(ahead2, ahead_pairs)
        column, top, rest = pl.pallas_call(
            lambda *refs: panel_head(tile, *refs),
            out_shape=(shape((rows, half), f32), shape((half, rows), f32), shape((half, rows), f32)),
            in_specs=[SMEM] + [VMEM] * 4, out_specs=(VMEM, ANY, ANY),
            scratch_shapes=[pltpu.VMEM((rows, tile), f32), pltpu.VMEM((tile, rows), f32), pltpu.VMEM((tile, rows), f32),
                            dma(2)],
            name="panel_head",
        )(panel, keep, got, mine, theirs)
        t1, t2, t3, column = hold((t1, t2, t3, column))
        out1 = sum(wide(value[:rows]) for value in (kept1, t1, t2, t3))
        own1 = sum(wide(value[rows:]) for value in (kept1, t1, t2, t3))
        beside, ahead1, top = hold((out1.astype(bf16), own1.astype(bf16), top))
        beside = move(beside, beside_pairs)
        ahead1 = move(ahead1, even_ahead_pairs)
        column, lower = pl.pallas_call(
            lambda *refs: panel_tail(tile, *refs),
            out_shape=(shape((rows, half), f32), shape((tile, tile), bf16)),
            in_specs=[SMEM, ANY, ANY, ANY], out_specs=(ANY, ANY), input_output_aliases={3: 0},
            scratch_shapes=[pltpu.VMEM((tile, rows), f32), pltpu.VMEM((tile, rows), f32), pltpu.VMEM((tile, tile), bf16),
                            pltpu.VMEM((rows, half), f32), dma(2)],
            name="panel_tail",
            compiler_params=pltpu.CompilerParams(vmem_limit_bytes=64 * 2**20 - 2**16),
        )(panel, top, rest, column)
        lower = move(lower, slab_pairs(2))
        out = pl.pallas_call(
            lambda *refs: final_kernel(tile, *refs),
            out_shape=shape((3, rows, half), f32),
            in_specs=[VMEM] * 6, out_specs=VMEM, name="assemble",
            compiler_params=pltpu.CompilerParams(vmem_limit_bytes=64 * 2**20 - 2**16),
        )(column, own2, own1, ahead2, ahead1, beside)
        out = pl.pallas_call(
            lambda *refs: reduce_kernel(tile, *refs),
            out_shape=shape((3, rows, half), f32),
            in_specs=[SMEM, ANY, ANY], out_specs=ANY, input_output_aliases={2: 0},
            scratch_shapes=[pltpu.VMEM((tile, tile), bf16), pltpu.VMEM((tile, half), f32), dma(3)], name="reduce",
        )(panel, lower, out)
        return out.transpose(1, 0, 2)

    return body


def solution(mesh):
    return jax.shard_map(
        make_body(mesh.shape["blk"], mesh.shape["slab"]),
        mesh=mesh,
        in_specs=(P("blk", "slab"), P("blk", "slab", None), P("blk", "slab"), P("slab"), P()),
        out_specs=P("blk", None, "slab"),
        check_vma=False,
    )
```

```python
import jax
import jax.numpy as jnp
from jax import lax
from jax.experimental import pallas as pl
from jax.experimental.pallas import tpu as pltpu
from jax.sharding import PartitionSpec as P

ridge_shift = 0.05
AXES = ("blk", "slab")
HIGH = lax.Precision.HIGHEST
SMEM = pl.BlockSpec(memory_space=pltpu.SMEM)
ANY = pl.BlockSpec(memory_space=pl.ANY)
VMEM = pl.BlockSpec(memory_space=pltpu.VMEM)


def product(lhs, rhs, lhs_cols, rhs_cols, scaling, table, scaled, tile, slots, col_tiles, emit):
    for b in range(2):
        for c in range(col_tiles):
            table[b, c] = jnp.int32(slots)
    for b in range(2):
        for n in range(slots):
            col = rhs_cols[b, n]
            table[b, col] = jnp.int32(n)

    def left(t, carry):
        i = t // slots
        m = t % slots
        col = lhs_cols[i, m]
        live = col < col_tiles
        col = jnp.minimum(col, col_tiles - 1)
        other = [table[b, col] for b in range(2)]

        @pl.when(live & ((other[0] < slots) | (other[1] < slots)))
        def _():
            rows = pl.ds(pl.multiple_of(i * tile, tile), tile)
            cols = pl.ds(pl.multiple_of(m * tile, tile), tile)
            scaled[...] = (lhs[rows, cols].astype(jnp.float32) * scaling[pl.ds(col, 1), :]).astype(jnp.bfloat16)
            for b in range(2):

                @pl.when(other[b] < slots)
                def _():
                    cols = pl.ds(pl.multiple_of(other[b] * tile, tile), tile)
                    emit(i, b, lax.dot_general(
                        scaled[...], rhs[b * tile:(b + 1) * tile, cols],
                        (((1,), (1,)), ((), ())), preferred_element_type=jnp.float32))

        return carry

    lax.fori_loop(0, 2 * slots, left, 0)


def live_cols(tile_cols, tile_counts, cols, slots, col_tiles):
    for b in range(2):
        for n in range(slots):
            cols[b, n] = jnp.where(n < tile_counts[b], tile_cols[b, 0, n], col_tiles)


def pack_kernel(slots, col_tiles, tile_cols, tile_counts, a, out, held, cols, tail, sems):
    pieces = 4
    rows = a.shape[0]
    size = rows // pieces
    part = [pl.ds(p * size, size) for p in range(pieces)]
    reads = [pltpu.make_async_copy(a.at[part[p], :], held.at[part[p], :], sems.at[p]) for p in range(pieces)]
    writes = [pltpu.make_async_copy(held.at[part[p], :], out.at[part[p], :], sems.at[pieces + p]) for p in range(pieces)]
    for copy in reads:
        copy.start()
    live_cols(tile_cols, tile_counts, cols, slots, col_tiles)
    row = lax.broadcasted_iota(jnp.int32, tail.shape, 0)
    lane = lax.broadcasted_iota(jnp.int32, tail.shape, 1)
    value = jnp.zeros(tail.shape, jnp.float32)
    for b in range(2):
        for n in range(slots):
            value = jnp.where((row == b) & (lane == n), cols[b, n].astype(jnp.float32), value)
    tail[...] = value.astype(tail.dtype)
    last = pltpu.make_async_copy(
        tail, out.at[pl.ds(rows, tail.shape[0]), pl.ds(0, tail.shape[1])], sems.at[2 * pieces])
    last.start()
    for read, write in zip(reads, writes):
        read.wait()
        write.start()
    for write in writes:
        write.wait()
    last.wait()


def tail_cols(packed, rows, tails, ints, cols, sems, first):
    count = len(packed)
    lists = [pltpu.make_async_copy(
        packed[n].at[pl.ds(rows, tails.shape[1]), pl.ds(0, tails.shape[2])], tails.at[n], sems.at[first + n])
        for n in range(count)]
    for copy in lists:
        copy.start()

    def finish():
        scalars = [pltpu.make_async_copy(ints.at[n], cols[n], sems.at[first + count + n]) for n in range(count)]
        for n in range(count):
            lists[n].wait()
            ints[n] = tails[n].astype(jnp.float32)[:ints.shape[1]].astype(jnp.int32)
            scalars[n].start()
        for copy in scalars:
            copy.wait()

    return finish


def own_kernel(tile, slots, col_tiles, tile_cols, tile_counts, scaling, a, give, keep, cols, table, scaled, acc):
    slab = lax.axis_index("slab")
    core = slab % 2
    y_lo = slab // 2
    rows = acc.shape[1]
    acc[...] = jnp.zeros_like(acc)
    live_cols(tile_cols, tile_counts, cols, slots, col_tiles)

    def emit(i, b, value):
        acc[b, pl.ds(pl.multiple_of(i * tile, tile), tile), :] += value

    product(a, a, cols, cols, scaling, table, scaled, tile, slots, col_tiles, emit)
    give[:rows, :] = acc[y_lo]
    keep[:rows, :] = acc[y_lo]
    give[rows:, :] = acc[1 - y_lo, pl.ds(pl.multiple_of((1 - core) * tile, tile), tile), :]
    keep[rows:, :] = acc[1 - y_lo, pl.ds(pl.multiple_of(core * tile, tile), tile), :]


def fetch(copies, sems):
    started = [pltpu.make_async_copy(src, dst, sems.at[n]) for n, (src, dst) in enumerate(copies)]
    for copy in started:
        copy.start()
    return started


def adder(acc, tile):
    half = tile // 2

    def emit(i, b, value):
        at = pl.ds(pl.multiple_of(i * tile, tile), tile)
        acc[2 * b, at, :] += value[:, :half]
        acc[2 * b + 1, at, :] += value[:, half:]

    return emit


def second_kernel(tile, slots, col_tiles, tile_cols, tile_counts, scaling, a_any, x_any, p1, p2, p3, kept,
                  a, x, cols, x_cols, tail, ints, table, scaled, acc, sems):
    slab = lax.axis_index("slab")
    core = slab % 2
    rows = a.shape[0]
    finish = tail_cols([x_any], rows, tail, ints, [x_cols], sems, 2)
    copies = fetch([(a_any, a), (x_any.at[pl.ds(0, rows), :], x)], sems)
    args = (scaling, table, scaled, tile, slots, col_tiles, adder(acc, tile))
    finish()
    live_cols(tile_cols, tile_counts, cols, slots, col_tiles)
    acc[...] = jnp.zeros_like(acc)
    for copy in copies:
        copy.wait()

    @pl.when(core == 0)
    def _():
        product(a, x, cols, x_cols, *args)

    @pl.when(core == 1)
    def _():
        product(x, a, x_cols, cols, *args)

    kept[...] = acc[slab]
    for k, ref in ((1, p1), (2, p2), (3, p3)):
        ref[...] = acc[slab ^ k].astype(ref.dtype)


def first_kernel(tile, slots, col_tiles, tile_cols, tile_counts, scaling, a_any, x_any, y_any, q1, q2, q3, kept,
                 a, x, y, cols, x_cols, y_cols, tail, ints, table, scaled, acc, sems):
    slab = lax.axis_index("slab")
    core = slab % 2
    hub = (core + lax.axis_index("blk")) % 2 == 1
    rows = a.shape[0]

    def store(start):
        kept[start:start + rows, :] = acc[slab]
        for k, ref in ((1, q1), (2, q2), (3, q3)):
            ref[start:start + rows, :] = acc[slab ^ k].astype(ref.dtype)

    @pl.when(jnp.logical_not(hub))
    def _():
        kept[...] = jnp.zeros_like(kept)

    @pl.when(hub)
    def _():
        part = pl.ds(0, rows)
        finish = tail_cols([x_any, y_any], rows, tail, ints, [x_cols, y_cols], sems, 3)
        y_copy = pltpu.make_async_copy(y_any.at[part, :], y, sems.at[0])
        x_copy = pltpu.make_async_copy(x_any.at[part, :], x, sems.at[1])
        a_copy = pltpu.make_async_copy(a_any, a, sems.at[2])
        y_copy.start()

        @pl.when(core == 0)
        def _():
            x_copy.start()
            a_copy.start()

        @pl.when(core == 1)
        def _():
            a_copy.start()
            x_copy.start()

        finish()
        live_cols(tile_cols, tile_counts, cols, slots, col_tiles)
        args = (scaling, table, scaled, tile, slots, col_tiles, adder(acc, tile))
        acc[...] = jnp.zeros_like(acc)
        y_copy.wait()

        @pl.when(core == 0)
        def _():
            x_copy.wait()
            product(y, x, y_cols, x_cols, *args)

        @pl.when(core == 1)
        def _():
            a_copy.wait()
            product(y, a, y_cols, cols, *args)

        store(0)
        acc[...] = jnp.zeros_like(acc)

        @pl.when(core == 0)
        def _():
            a_copy.wait()
            product(a, y, cols, y_cols, *args)

        @pl.when(core == 1)
        def _():
            x_copy.wait()
            product(x, y, x_cols, y_cols, *args)

        store(rows)


def eliminate(matrix, size, group):
    tiles = size // 8
    v = matrix.reshape(tiles, 8, 128)
    ids = lax.broadcasted_iota(jnp.int32, (tiles, 8, 128), 0) * 8 + lax.broadcasted_iota(
        jnp.int32, (tiles, 8, 128), 1)
    pivots = [jnp.ones((8, 128), jnp.float32) for _ in range(tiles)]
    for j in range(0, size, group):
        s = {}
        for a in range(group):
            for b in range(a + 1):
                r = j + a
                s[a, b] = jnp.broadcast_to(v[r // 8, r % 8:r % 8 + 1, j + b:j + b + 1], (8, 128))
        rows = [jnp.broadcast_to(v[(j + a) // 8, (j + a) % 8:(j + a) % 8 + 1, :], (8, 128)) for a in range(group)]
        below = (j + group) // 8
        last = j + group >= size
        cols = [] if last else [
            jnp.broadcast_to(v[below:, :, j + b:j + b + 1], (tiles - below, 8, 128)) for b in range(group)]
        low = {}
        inverse = []
        for b in range(group):
            inverse.append(1.0 / s[b, b])
            for a in range(b + 1, group):
                low[a, b] = s[a, b] * inverse[b]
            for a in range(b + 1, group):
                for c in range(b + 1, a + 1):
                    s[a, c] = s[a, c] - low[a, b] * s[c, b]
        for a in range(group):
            for b in range(a):
                rows[a] = rows[a] - low[a, b] * rows[b]
        top = j // 8
        kept = v[top]
        for a in range(group):
            here = ids[top] == j + a
            kept = jnp.where(here, rows[a], kept)
            pivots[top] = jnp.where(here, s[a, a], pivots[top])
        pieces = [v[:top]] if top else []
        pieces.append(kept[None])
        if not last:
            steps = []
            update = None
            for b in range(group):
                step = cols[b]
                for k in range(b):
                    step = step - steps[k] * s[b, k][None]
                steps.append(step * inverse[b][None])
                term = steps[b] * rows[b][None]
                update = term if update is None else update + term
            pieces.append(v[below:] - update)
        v = jnp.concatenate(pieces, 0) if len(pieces) > 1 else pieces[0]
    return (v * lax.rsqrt(jnp.stack(pivots))).reshape(size, 128)


def panel_factor(w, u, first, stop, size, group):
    n, width = w.shape
    for start in range(first, stop, size):
        base = start // 128 * 128
        square = w[start:start + size, base:base + 128]
        if start > base:
            square = pltpu.roll(square, 128 - (start - base), 1)
        lane = lax.broadcasted_iota(jnp.int32, (size, 128), 1)
        row = lax.broadcasted_iota(jnp.int32, (size, 128), 0)
        square = jnp.where(lane < size, square, jnp.where(lane - size == row, 1.0, 0.0))
        inverse = eliminate(square, size, group)[:, size:2 * size]
        strip = lax.dot_general(
            inverse, w[start:start + size, :], (((1,), (0,)), ((), ())),
            precision=HIGH, preferred_element_type=jnp.float32)
        lane = lax.broadcasted_iota(jnp.int32, (size, width), 1)
        row = lax.broadcasted_iota(jnp.int32, (size, width), 0)
        strip = jnp.where(lane - start >= row, strip, 0.0)
        u[start:start + size, :] = strip
        if start + size < n:
            w[start + size:, :] = w[start + size:, :] - lax.dot_general(
                strip[:, start + size:n], strip, (((0,), (0,)), ((), ())),
                precision=HIGH, preferred_element_type=jnp.float32)


def holds_panel(panel):
    block = panel[0]
    pos = block % 2
    return (block // 2 == lax.axis_index("blk")) & (pos == lax.axis_index("slab") // 2), pos


def panel_head(tile, panel, keep, got, mine, theirs, column, top, rest, total, w, u, sems):
    slab = lax.axis_index("slab")
    core = slab % 2
    y_lo = slab // 2
    half = tile // 2
    holds, pos = holds_panel(panel)
    rows = total.shape[0]
    total[...] = keep[:rows, :] + got[:rows, :]
    total[pl.ds(pl.multiple_of(core * tile, tile), tile), :] += mine[...]
    total[pl.ds(pl.multiple_of((1 - core) * tile, tile), tile), :] += theirs[...]
    eye = jnp.where(
        lax.broadcasted_iota(jnp.int32, (tile, tile), 0) == lax.broadcasted_iota(jnp.int32, (tile, tile), 1),
        jnp.float32(ridge_shift), jnp.float32(0.0))
    total[pl.ds(pl.multiple_of(y_lo * tile, tile), tile), :] += eye

    @pl.when(core == 0)
    def _():
        column[...] = total[:, :half]

    @pl.when(core == 1)
    def _():
        column[...] = total[:, half:]

    @pl.when(holds)
    def _():
        square = total[pl.ds(pl.multiple_of(pos * tile, tile), tile), :]
        w[:, :tile] = (square + square.T) * 0.5
        w[:, tile:] = total[pl.ds(pl.multiple_of((1 - pos) * tile, tile), tile), :].T
        panel_factor(w, u, 0, half, 64, 8)
        for copy in fetch([(u.at[pl.ds(0, half), :], top), (w.at[pl.ds(half, half), :], rest)], sems):
            copy.wait()


def panel_tail(tile, panel, top, rest, before, column, lower, w, u, low, mine, sems):
    core = lax.axis_index("slab") % 2
    half = tile // 2
    holds, pos = holds_panel(panel)

    @pl.when(holds)
    def _():
        for copy in fetch([(top, u.at[pl.ds(0, half), :]), (rest, w.at[pl.ds(half, half), :])], sems):
            copy.wait()
        panel_factor(w, u, half, tile, 64, 8)
        low[...] = u[:, tile:].astype(low.dtype)
        out = pltpu.make_async_copy(low, lower, sems.at[0])
        out.start()
        rows = pl.ds(pl.multiple_of(core * half, half), half)
        mine[pl.ds(pl.multiple_of(pos * tile, tile), tile), :] = u[rows, :tile].T
        mine[pl.ds(pl.multiple_of((1 - pos) * tile, tile), tile), :] = u[rows, tile:].T
        back = pltpu.make_async_copy(mine, column, sems.at[1])
        back.start()
        out.wait()
        back.wait()


def final_kernel(tile, column, own2, own1, ahead2, ahead1, beside, out):
    group = lax.axis_index("blk")
    rows = column.shape[0]
    out[0] = column[...]
    out[2] = own2[...] + ahead2[...].astype(jnp.float32)
    late = jnp.where(group % 2 == 1, own1[...], ahead1[...].astype(jnp.float32))
    out[1] = late + beside[...].astype(jnp.float32)


def reduce_kernel(tile, panel, lower_any, band, out, lower, corner, sems):
    slab = lax.axis_index("slab")
    core = slab % 2
    y_lo = slab // 2
    half = tile // 2
    block = panel[0]

    @pl.when((block // 2 == lax.axis_index("blk")) & (block % 2 != y_lo))
    def _():
        here = out.at[0, pl.ds(pl.multiple_of(y_lo * tile, tile), tile), :]
        for copy in fetch([(lower_any, lower), (here, corner)], sems):
            copy.wait()
        left = lower[...].astype(jnp.float32)
        right = jnp.where(core == 0, left[:, :half], left[:, half:])
        corner[...] = corner[...] - lax.dot_general(
            left, right, (((0,), (0,)), ((), ())), precision=HIGH, preferred_element_type=jnp.float32)
        back = pltpu.make_async_copy(corner, here, sems.at[2])
        back.start()
        back.wait()


def make_body(groups, slabs):
    devices = [(g, s) for g in range(groups) for s in range(slabs)]
    at = lambda g, s: (g % groups) * slabs + s
    forward = lambda s: s % 2 == 0
    hubs = [(g, s) for g, s in devices if (g + s) % 2 == 1]
    far_pairs = [(at(g, s), at(g + (2 if forward(s) else -2), s)) for g, s in devices]
    near_pairs = [(at(g + (-1 if forward(s) else 1), s), at(g, s)) for g, s in hubs]
    slab_pairs = lambda k, among=devices: [(at(g, s), at(g, s ^ k)) for g, s in among]
    ahead_pairs = [(at(g, s), at(g + 2, s)) for g, s in devices]
    even_ahead_pairs = [(at(g, s), at(g + 2, s)) for g, s in devices if g % 2 == 0]
    beside_pairs = [(at(g, s), at(g ^ 1, s)) for g, s in devices]

    hold = lax.optimization_barrier

    def move(value, pairs):
        return lax.ppermute(value, AXES, pairs)

    def body(a_tiles, tile_cols, tile_counts, scaling, panel):
        rows = a_tiles.shape[0]
        blocks = tile_cols.shape[0]
        slots = tile_cols.shape[2]
        tile = rows // blocks
        col_tiles = scaling.shape[0] // tile
        half = tile // 2
        f32 = jnp.float32
        bf16 = jnp.bfloat16
        shape = jax.ShapeDtypeStruct
        scales = scaling.reshape(col_tiles, tile)
        cols = pltpu.SMEM((2, slots), jnp.int32)
        tail = pltpu.VMEM((16, 128), bf16)
        counts = tile_counts[:, 0]
        moved = pltpu.SMEM((8, 128), jnp.int32)
        dma = lambda n: pltpu.SemaphoreType.DMA((n,))
        packed = pl.pallas_call(
            lambda *refs: pack_kernel(slots, col_tiles, *refs),
            out_shape=shape((rows + 16, a_tiles.shape[1]), bf16),
            in_specs=[SMEM, SMEM, ANY], out_specs=ANY, scratch_shapes=[pltpu.VMEM(a_tiles.shape, bf16), cols, tail, dma(9)], name="pack",
        )(tile_cols, counts, a_tiles)
        table = pltpu.SMEM((2, col_tiles + 1), jnp.int32)
        scaled = pltpu.VMEM((tile, tile), bf16)
        sizes = (tile, slots, col_tiles)
        own_tiles, packed = hold((a_tiles, packed))
        x = move(packed, far_pairs)
        y = move(packed, near_pairs)
        give, keep = pl.pallas_call(
            lambda *refs: own_kernel(*sizes, *refs),
            out_shape=(shape((rows + tile, tile), f32), shape((rows + tile, tile), f32)),
            in_specs=[SMEM, SMEM, VMEM, VMEM], out_specs=(VMEM, VMEM),
            scratch_shapes=[cols, table, scaled, pltpu.VMEM((2, rows, tile), f32)], name="plane_zero",
            compiler_params=pltpu.CompilerParams(vmem_limit_bytes=64 * 2**20 - 2**16),
        )(tile_cols, counts, scales, own_tiles)
        got = move(give, slab_pairs(1))
        mine = move(keep[rows:] + got[rows:], slab_pairs(2))
        part = shape((rows, half), bf16)
        two = shape((2 * rows, half), bf16)
        whole = pltpu.VMEM(a_tiles.shape, bf16)
        acc = pltpu.VMEM((4, rows, half), f32)
        p1, p2, p3, kept2 = pl.pallas_call(
            lambda *refs: second_kernel(*sizes, *refs),
            out_shape=(part, part, part, shape((rows, half), f32)),
            in_specs=[SMEM, SMEM, VMEM, ANY, ANY], out_specs=(VMEM,) * 4,
            scratch_shapes=[whole, whole, cols, moved, pltpu.VMEM((1, 16, 128), bf16), pltpu.VMEM((1, 8, 128), jnp.int32), table, scaled, acc, dma(4)],
            name="plane_two",
        )(tile_cols, counts, scales, a_tiles, x)
        y, kept2 = hold((y, kept2))
        q1, q2, q3, kept1 = pl.pallas_call(
            lambda *refs: first_kernel(*sizes, *refs),
            out_shape=(two, two, two, shape((2 * rows, half), f32)),
            in_specs=[SMEM, SMEM, VMEM, ANY, ANY, ANY], out_specs=(VMEM,) * 4,
            scratch_shapes=[whole, whole, whole, cols, moved, moved, pltpu.VMEM((2, 16, 128), bf16), pltpu.VMEM((2, 8, 128), jnp.int32), table, scaled, acc, dma(7)],
            name="plane_one",
        )(tile_cols, counts, scales, a_tiles, x, y)
        r1, r2, r3 = [move(p, slab_pairs(k)) for k, p in ((1, p1), (2, p2), (3, p3))]
        t1, t2, t3 = [move(q, slab_pairs(k, hubs)) for k, q in ((1, q1), (2, q2), (3, q3))]
        core = lax.axis_index("slab") % 2
        wide = lambda value: value.astype(f32)
        r1, r2, r3, mine = hold((r1, r2, r3, mine))
        theirs = move(mine, slab_pairs(1))
        same = kept2 + wide(r2)
        swapped = wide(r1) + wide(r3)
        own2 = jnp.where(core == 0, same, swapped)
        ahead2 = jnp.where(core == 0, swapped, same).astype(bf16)
        column, top, rest = pl.pallas_call(
            lambda *refs: panel_head(tile, *refs),
            out_shape=(shape((rows, half), f32), shape((half, rows), f32), shape((half, rows), f32)),
            in_specs=[SMEM] + [VMEM] * 4, out_specs=(VMEM, ANY, ANY),
            scratch_shapes=[pltpu.VMEM((rows, tile), f32), pltpu.VMEM((tile, rows), f32), pltpu.VMEM((tile, rows), f32),
                            dma(2)],
            name="panel_head",
        )(panel, keep, got, mine, theirs)
        t1, t2, t3, column, ahead2 = hold((t1, t2, t3, column, ahead2))
        ahead2 = move(ahead2, ahead_pairs)
        out1 = sum(wide(value[:rows]) for value in (kept1, t1, t2, t3))
        own1 = sum(wide(value[rows:]) for value in (kept1, t1, t2, t3))
        beside, ahead1, top = hold((out1.astype(bf16), own1.astype(bf16), top))
        beside = move(beside, beside_pairs)
        ahead1 = move(ahead1, even_ahead_pairs)
        column, lower = pl.pallas_call(
            lambda *refs: panel_tail(tile, *refs),
            out_shape=(shape((rows, half), f32), shape((tile, tile), bf16)),
            in_specs=[SMEM, ANY, ANY, ANY], out_specs=(ANY, ANY), input_output_aliases={3: 0},
            scratch_shapes=[pltpu.VMEM((tile, rows), f32), pltpu.VMEM((tile, rows), f32), pltpu.VMEM((tile, tile), bf16),
                            pltpu.VMEM((rows, half), f32), dma(2)],
            name="panel_tail",
            compiler_params=pltpu.CompilerParams(vmem_limit_bytes=64 * 2**20 - 2**16),
        )(panel, top, rest, column)
        lower = move(lower, slab_pairs(2))
        out = pl.pallas_call(
            lambda *refs: final_kernel(tile, *refs),
            out_shape=shape((3, rows, half), f32),
            in_specs=[VMEM] * 6, out_specs=VMEM, name="assemble",
            compiler_params=pltpu.CompilerParams(vmem_limit_bytes=64 * 2**20 - 2**16),
        )(column, own2, own1, ahead2, ahead1, beside)
        out = pl.pallas_call(
            lambda *refs: reduce_kernel(tile, *refs),
            out_shape=shape((3, rows, half), f32),
            in_specs=[SMEM, ANY, ANY], out_specs=ANY, input_output_aliases={2: 0},
            scratch_shapes=[pltpu.VMEM((tile, tile), bf16), pltpu.VMEM((tile, half), f32), dma(3)], name="reduce",
        )(panel, lower, out)
        return out.transpose(1, 0, 2)

    return body


def solution(mesh):
    return jax.shard_map(
        make_body(mesh.shape["blk"], mesh.shape["slab"]),
        mesh=mesh,
        in_specs=(P("blk", "slab"), P("blk", "slab", None), P("blk", "slab"), P("slab"), P()),
        out_specs=P("blk", None, "slab"),
        check_vma=False,
    )
```

```python
import jax
import jax.numpy as jnp
from jax import lax
from jax.experimental import pallas as pl
from jax.experimental.pallas import tpu as pltpu
from jax.sharding import PartitionSpec as P

ridge_shift = 0.05
AXES = ("blk", "slab")
HIGH = lax.Precision.HIGHEST
SMEM = pl.BlockSpec(memory_space=pltpu.SMEM)
ANY = pl.BlockSpec(memory_space=pl.ANY)
VMEM = pl.BlockSpec(memory_space=pltpu.VMEM)


def product(lhs, rhs, lhs_cols, rhs_cols, scaling, table, scaled, tile, slots, col_tiles, emit):
    for b in range(2):
        for c in range(col_tiles):
            table[b, c] = jnp.int32(slots)
    for b in range(2):
        for n in range(slots):
            col = rhs_cols[b, n]
            table[b, col] = jnp.int32(n)

    def left(t, carry):
        i = t // slots
        m = t % slots
        col = lhs_cols[i, m]
        live = col < col_tiles
        col = jnp.minimum(col, col_tiles - 1)
        other = [table[b, col] for b in range(2)]

        @pl.when(live & ((other[0] < slots) | (other[1] < slots)))
        def _():
            rows = pl.ds(pl.multiple_of(i * tile, tile), tile)
            cols = pl.ds(pl.multiple_of(m * tile, tile), tile)
            scaled[...] = (lhs[rows, cols].astype(jnp.float32) * scaling[pl.ds(col, 1), :]).astype(jnp.bfloat16)
            for b in range(2):

                @pl.when(other[b] < slots)
                def _():
                    cols = pl.ds(pl.multiple_of(other[b] * tile, tile), tile)
                    emit(i, b, lax.dot_general(
                        scaled[...], rhs[b * tile:(b + 1) * tile, cols],
                        (((1,), (1,)), ((), ())), preferred_element_type=jnp.float32))

        return carry

    lax.fori_loop(0, 2 * slots, left, 0)


def live_cols(tile_cols, tile_counts, cols, slots, col_tiles):
    for b in range(2):
        for n in range(slots):
            cols[b, n] = jnp.where(n < tile_counts[b], tile_cols[b, 0, n], col_tiles)


def pack_kernel(slots, col_tiles, tile_cols, tile_counts, a, out, held, cols, tail, sems):
    pieces = 4
    rows = a.shape[0]
    size = rows // pieces
    part = [pl.ds(p * size, size) for p in range(pieces)]
    reads = [pltpu.make_async_copy(a.at[part[p], :], held.at[part[p], :], sems.at[p]) for p in range(pieces)]
    writes = [pltpu.make_async_copy(held.at[part[p], :], out.at[part[p], :], sems.at[pieces + p]) for p in range(pieces)]
    for copy in reads:
        copy.start()
    live_cols(tile_cols, tile_counts, cols, slots, col_tiles)
    row = lax.broadcasted_iota(jnp.int32, tail.shape, 0)
    lane = lax.broadcasted_iota(jnp.int32, tail.shape, 1)
    value = jnp.zeros(tail.shape, jnp.float32)
    for b in range(2):
        for n in range(slots):
            value = jnp.where((row == b) & (lane == n), cols[b, n].astype(jnp.float32), value)
    tail[...] = value.astype(tail.dtype)
    last = pltpu.make_async_copy(
        tail, out.at[pl.ds(rows, tail.shape[0]), pl.ds(0, tail.shape[1])], sems.at[2 * pieces])
    last.start()
    for read, write in zip(reads, writes):
        read.wait()
        write.start()
    for write in writes:
        write.wait()
    last.wait()


def tail_cols(packed, rows, tails, ints, cols, sems, first):
    count = len(packed)
    lists = [pltpu.make_async_copy(
        packed[n].at[pl.ds(rows, tails.shape[1]), pl.ds(0, tails.shape[2])], tails.at[n], sems.at[first + n])
        for n in range(count)]
    for copy in lists:
        copy.start()

    def finish():
        scalars = [pltpu.make_async_copy(ints.at[n], cols[n], sems.at[first + count + n]) for n in range(count)]
        for n in range(count):
            lists[n].wait()
            ints[n] = tails[n].astype(jnp.float32)[:ints.shape[1]].astype(jnp.int32)
            scalars[n].start()
        for copy in scalars:
            copy.wait()

    return finish


def own_kernel(tile, slots, col_tiles, tile_cols, tile_counts, scaling, a, give, keep, cols, table, scaled, acc):
    slab = lax.axis_index("slab")
    core = slab % 2
    y_lo = slab // 2
    rows = acc.shape[1]
    acc[...] = jnp.zeros_like(acc)
    live_cols(tile_cols, tile_counts, cols, slots, col_tiles)

    def emit(i, b, value):
        acc[b, pl.ds(pl.multiple_of(i * tile, tile), tile), :] += value

    product(a, a, cols, cols, scaling, table, scaled, tile, slots, col_tiles, emit)
    give[:rows, :] = acc[y_lo]
    keep[:rows, :] = acc[y_lo]
    give[rows:, :] = acc[1 - y_lo, pl.ds(pl.multiple_of((1 - core) * tile, tile), tile), :]
    keep[rows:, :] = acc[1 - y_lo, pl.ds(pl.multiple_of(core * tile, tile), tile), :]


def fetch(copies, sems):
    started = [pltpu.make_async_copy(src, dst, sems.at[n]) for n, (src, dst) in enumerate(copies)]
    for copy in started:
        copy.start()
    return started


def adder(acc, tile):
    half = tile // 2

    def emit(i, b, value):
        at = pl.ds(pl.multiple_of(i * tile, tile), tile)
        acc[2 * b, at, :] += value[:, :half]
        acc[2 * b + 1, at, :] += value[:, half:]

    return emit


def second_kernel(tile, slots, col_tiles, tile_cols, tile_counts, scaling, a_any, x_any, p1, p2, p3, kept,
                  a, x, cols, x_cols, tail, ints, table, scaled, acc, sems):
    slab = lax.axis_index("slab")
    core = slab % 2
    rows = a.shape[0]
    finish = tail_cols([x_any], rows, tail, ints, [x_cols], sems, 2)
    copies = fetch([(a_any, a), (x_any.at[pl.ds(0, rows), :], x)], sems)
    args = (scaling, table, scaled, tile, slots, col_tiles, adder(acc, tile))
    finish()
    live_cols(tile_cols, tile_counts, cols, slots, col_tiles)
    acc[...] = jnp.zeros_like(acc)
    for copy in copies:
        copy.wait()

    @pl.when(core == 0)
    def _():
        product(a, x, cols, x_cols, *args)

    @pl.when(core == 1)
    def _():
        product(x, a, x_cols, cols, *args)

    kept[...] = acc[slab]
    for k, ref in ((1, p1), (2, p2), (3, p3)):
        ref[...] = acc[slab ^ k].astype(ref.dtype)


def first_kernel(tile, slots, col_tiles, tile_cols, tile_counts, scaling, a_any, x_any, y_any, q1, q2, q3, kept,
                 a, x, y, cols, x_cols, y_cols, tail, ints, table, scaled, acc, sems):
    slab = lax.axis_index("slab")
    core = slab % 2
    hub = (core + lax.axis_index("blk")) % 2 == 1
    rows = a.shape[0]

    def store(start):
        kept[start:start + rows, :] = acc[slab]
        for k, ref in ((1, q1), (2, q2), (3, q3)):
            ref[start:start + rows, :] = acc[slab ^ k].astype(ref.dtype)

    @pl.when(jnp.logical_not(hub))
    def _():
        kept[...] = jnp.zeros_like(kept)

    @pl.when(hub)
    def _():
        part = pl.ds(0, rows)
        finish = tail_cols([x_any, y_any], rows, tail, ints, [x_cols, y_cols], sems, 3)
        y_copy = pltpu.make_async_copy(y_any.at[part, :], y, sems.at[0])
        x_copy = pltpu.make_async_copy(x_any.at[part, :], x, sems.at[1])
        a_copy = pltpu.make_async_copy(a_any, a, sems.at[2])
        y_copy.start()

        @pl.when(core == 0)
        def _():
            x_copy.start()
            a_copy.start()

        @pl.when(core == 1)
        def _():
            a_copy.start()
            x_copy.start()

        finish()
        live_cols(tile_cols, tile_counts, cols, slots, col_tiles)
        args = (scaling, table, scaled, tile, slots, col_tiles, adder(acc, tile))
        acc[...] = jnp.zeros_like(acc)
        y_copy.wait()

        @pl.when(core == 0)
        def _():
            x_copy.wait()
            product(y, x, y_cols, x_cols, *args)

        @pl.when(core == 1)
        def _():
            a_copy.wait()
            product(y, a, y_cols, cols, *args)

        store(0)
        acc[...] = jnp.zeros_like(acc)

        @pl.when(core == 0)
        def _():
            a_copy.wait()
            product(a, y, cols, y_cols, *args)

        @pl.when(core == 1)
        def _():
            x_copy.wait()
            product(x, y, x_cols, y_cols, *args)

        store(rows)


def eliminate(matrix, size, group):
    tiles = size // 8
    v = matrix.reshape(tiles, 8, 128)
    ids = lax.broadcasted_iota(jnp.int32, (tiles, 8, 128), 0) * 8 + lax.broadcasted_iota(
        jnp.int32, (tiles, 8, 128), 1)
    pivots = [jnp.ones((8, 128), jnp.float32) for _ in range(tiles)]
    for j in range(0, size, group):
        s = {}
        for a in range(group):
            for b in range(a + 1):
                r = j + a
                s[a, b] = jnp.broadcast_to(v[r // 8, r % 8:r % 8 + 1, j + b:j + b + 1], (8, 128))
        rows = [jnp.broadcast_to(v[(j + a) // 8, (j + a) % 8:(j + a) % 8 + 1, :], (8, 128)) for a in range(group)]
        below = (j + group) // 8
        last = j + group >= size
        cols = [] if last else [
            jnp.broadcast_to(v[below:, :, j + b:j + b + 1], (tiles - below, 8, 128)) for b in range(group)]
        low = {}
        inverse = []
        for b in range(group):
            inverse.append(1.0 / s[b, b])
            for a in range(b + 1, group):
                low[a, b] = s[a, b] * inverse[b]
            for a in range(b + 1, group):
                for c in range(b + 1, a + 1):
                    s[a, c] = s[a, c] - low[a, b] * s[c, b]
        for a in range(group):
            for b in range(a):
                rows[a] = rows[a] - low[a, b] * rows[b]
        top = j // 8
        kept = v[top]
        for a in range(group):
            here = ids[top] == j + a
            kept = jnp.where(here, rows[a], kept)
            pivots[top] = jnp.where(here, s[a, a], pivots[top])
        pieces = [v[:top]] if top else []
        pieces.append(kept[None])
        if not last:
            steps = []
            update = None
            for b in range(group):
                step = cols[b]
                for k in range(b):
                    step = step - steps[k] * s[b, k][None]
                steps.append(step * inverse[b][None])
                term = steps[b] * rows[b][None]
                update = term if update is None else update + term
            pieces.append(v[below:] - update)
        v = jnp.concatenate(pieces, 0) if len(pieces) > 1 else pieces[0]
    return (v * lax.rsqrt(jnp.stack(pivots))).reshape(size, 128)


def panel_factor(w, u, first, stop, size, group):
    n, width = w.shape
    for start in range(first, stop, size):
        base = start // 128 * 128
        square = w[start:start + size, base:base + 128]
        if start > base:
            square = pltpu.roll(square, 128 - (start - base), 1)
        lane = lax.broadcasted_iota(jnp.int32, (size, 128), 1)
        row = lax.broadcasted_iota(jnp.int32, (size, 128), 0)
        square = jnp.where(lane < size, square, jnp.where(lane - size == row, 1.0, 0.0))
        inverse = eliminate(square, size, group)[:, size:2 * size]
        strip = lax.dot_general(
            inverse, w[start:start + size, :], (((1,), (0,)), ((), ())),
            precision=HIGH, preferred_element_type=jnp.float32)
        lane = lax.broadcasted_iota(jnp.int32, (size, width), 1)
        row = lax.broadcasted_iota(jnp.int32, (size, width), 0)
        strip = jnp.where(lane - start >= row, strip, 0.0)
        u[start:start + size, :] = strip
        if start + size < n:
            w[start + size:, :] = w[start + size:, :] - lax.dot_general(
                strip[:, start + size:n], strip, (((0,), (0,)), ((), ())),
                precision=HIGH, preferred_element_type=jnp.float32)


def holds_panel(panel):
    block = panel[0]
    pos = block % 2
    return (block // 2 == lax.axis_index("blk")) & (pos == lax.axis_index("slab") // 2), pos


def panel_head(tile, panel, keep, got, mine, theirs, column, top, rest, total, w, u, sems):
    slab = lax.axis_index("slab")
    core = slab % 2
    y_lo = slab // 2
    half = tile // 2
    holds, pos = holds_panel(panel)
    rows = total.shape[0]
    total[...] = keep[:rows, :] + got[:rows, :]
    total[pl.ds(pl.multiple_of(core * tile, tile), tile), :] += mine[...]
    total[pl.ds(pl.multiple_of((1 - core) * tile, tile), tile), :] += theirs[...]
    eye = jnp.where(
        lax.broadcasted_iota(jnp.int32, (tile, tile), 0) == lax.broadcasted_iota(jnp.int32, (tile, tile), 1),
        jnp.float32(ridge_shift), jnp.float32(0.0))
    total[pl.ds(pl.multiple_of(y_lo * tile, tile), tile), :] += eye

    @pl.when(core == 0)
    def _():
        column[...] = total[:, :half]

    @pl.when(core == 1)
    def _():
        column[...] = total[:, half:]

    @pl.when(holds)
    def _():
        square = total[pl.ds(pl.multiple_of(pos * tile, tile), tile), :]
        w[:, :tile] = (square + square.T) * 0.5
        w[:, tile:] = total[pl.ds(pl.multiple_of((1 - pos) * tile, tile), tile), :].T
        panel_factor(w, u, 0, half, 64, 8)
        for copy in fetch([(u.at[pl.ds(0, half), :], top), (w.at[pl.ds(half, half), :], rest)], sems):
            copy.wait()


def panel_tail(tile, panel, top, rest, before, column, lower, w, u, low, mine, sems):
    core = lax.axis_index("slab") % 2
    half = tile // 2
    holds, pos = holds_panel(panel)

    @pl.when(holds)
    def _():
        for copy in fetch([(top, u.at[pl.ds(0, half), :]), (rest, w.at[pl.ds(half, half), :])], sems):
            copy.wait()
        panel_factor(w, u, half, tile, 64, 8)
        low[...] = u[:, tile:].astype(low.dtype)
        out = pltpu.make_async_copy(low, lower, sems.at[0])
        out.start()
        rows = pl.ds(pl.multiple_of(core * half, half), half)
        mine[pl.ds(pl.multiple_of(pos * tile, tile), tile), :] = u[rows, :tile].T
        mine[pl.ds(pl.multiple_of((1 - pos) * tile, tile), tile), :] = u[rows, tile:].T
        back = pltpu.make_async_copy(mine, column, sems.at[1])
        back.start()
        out.wait()
        back.wait()


def final_kernel(tile, column, own2, own1, ahead2, ahead1, beside, out):
    group = lax.axis_index("blk")
    rows = column.shape[0]
    out[0] = column[...]
    out[2] = own2[...] + ahead2[...].astype(jnp.float32)
    late = jnp.where(group % 2 == 1, own1[...], ahead1[...].astype(jnp.float32))
    out[1] = late + beside[...].astype(jnp.float32)


def reduce_kernel(tile, panel, lower_any, band, out, lower, corner, sems):
    slab = lax.axis_index("slab")
    core = slab % 2
    y_lo = slab // 2
    half = tile // 2
    block = panel[0]

    @pl.when((block // 2 == lax.axis_index("blk")) & (block % 2 != y_lo))
    def _():
        here = out.at[0, pl.ds(pl.multiple_of(y_lo * tile, tile), tile), :]
        for copy in fetch([(lower_any, lower), (here, corner)], sems):
            copy.wait()
        left = lower[...].astype(jnp.float32)
        right = jnp.where(core == 0, left[:, :half], left[:, half:])
        corner[...] = corner[...] - lax.dot_general(
            left, right, (((0,), (0,)), ((), ())), precision=HIGH, preferred_element_type=jnp.float32)
        back = pltpu.make_async_copy(corner, here, sems.at[2])
        back.start()
        back.wait()


def make_body(groups, slabs):
    devices = [(g, s) for g in range(groups) for s in range(slabs)]
    at = lambda g, s: (g % groups) * slabs + s
    forward = lambda s: s % 2 == 0
    hubs = [(g, s) for g, s in devices if (g + s) % 2 == 1]
    far_pairs = [(at(g, s), at(g + (2 if forward(s) else -2), s)) for g, s in devices]
    near_pairs = [(at(g + (-1 if forward(s) else 1), s), at(g, s)) for g, s in hubs]
    slab_pairs = lambda k, among=devices: [(at(g, s), at(g, s ^ k)) for g, s in among]
    ahead_pairs = [(at(g, s), at(g + 2, s)) for g, s in devices]
    even_ahead_pairs = [(at(g, s), at(g + 2, s)) for g, s in devices if g % 2 == 0]
    beside_pairs = [(at(g, s), at(g ^ 1, s)) for g, s in devices]

    hold = lax.optimization_barrier

    def move(value, pairs):
        return lax.ppermute(value, AXES, pairs)

    def body(a_tiles, tile_cols, tile_counts, scaling, panel):
        rows = a_tiles.shape[0]
        blocks = tile_cols.shape[0]
        slots = tile_cols.shape[2]
        tile = rows // blocks
        col_tiles = scaling.shape[0] // tile
        half = tile // 2
        f32 = jnp.float32
        bf16 = jnp.bfloat16
        shape = jax.ShapeDtypeStruct
        scales = scaling.reshape(col_tiles, tile)
        cols = pltpu.SMEM((2, slots), jnp.int32)
        tail = pltpu.VMEM((16, 128), bf16)
        counts = tile_counts[:, 0]
        moved = pltpu.SMEM((8, 128), jnp.int32)
        dma = lambda n: pltpu.SemaphoreType.DMA((n,))
        packed = pl.pallas_call(
            lambda *refs: pack_kernel(slots, col_tiles, *refs),
            out_shape=shape((rows + 16, a_tiles.shape[1]), bf16),
            in_specs=[SMEM, SMEM, ANY], out_specs=ANY, scratch_shapes=[pltpu.VMEM(a_tiles.shape, bf16), cols, tail, dma(9)], name="pack",
        )(tile_cols, counts, a_tiles)
        table = pltpu.SMEM((2, col_tiles + 1), jnp.int32)
        scaled = pltpu.VMEM((tile, tile), bf16)
        sizes = (tile, slots, col_tiles)
        own_tiles, packed = hold((a_tiles, packed))
        x = move(packed, far_pairs)
        y = move(packed, near_pairs)
        give, keep = pl.pallas_call(
            lambda *refs: own_kernel(*sizes, *refs),
            out_shape=(shape((rows + tile, tile), f32), shape((rows + tile, tile), f32)),
            in_specs=[SMEM, SMEM, VMEM, VMEM], out_specs=(VMEM, VMEM),
            scratch_shapes=[cols, table, scaled, pltpu.VMEM((2, rows, tile), f32)], name="plane_zero",
            compiler_params=pltpu.CompilerParams(vmem_limit_bytes=64 * 2**20 - 2**16),
        )(tile_cols, counts, scales, own_tiles)
        got = move(give, slab_pairs(1))
        mine = move(keep[rows:] + got[rows:], slab_pairs(2))
        part = shape((rows, half), bf16)
        two = shape((2 * rows, half), bf16)
        whole = pltpu.VMEM(a_tiles.shape, bf16)
        acc = pltpu.VMEM((4, rows, half), f32)
        p1, p2, p3, kept2 = pl.pallas_call(
            lambda *refs: second_kernel(*sizes, *refs),
            out_shape=(part, part, part, shape((rows, half), f32)),
            in_specs=[SMEM, SMEM, VMEM, ANY, ANY], out_specs=(VMEM,) * 4,
            scratch_shapes=[whole, whole, cols, moved, pltpu.VMEM((1, 16, 128), bf16), pltpu.VMEM((1, 8, 128), jnp.int32), table, scaled, acc, dma(4)],
            name="plane_two",
            compiler_params=pltpu.CompilerParams(vmem_limit_bytes=64 * 2**20 - 2**16),
        )(tile_cols, counts, scales, a_tiles, x)
        y, kept2 = hold((y, kept2))
        q1, q2, q3, kept1 = pl.pallas_call(
            lambda *refs: first_kernel(*sizes, *refs),
            out_shape=(two, two, two, shape((2 * rows, half), f32)),
            in_specs=[SMEM, SMEM, VMEM, ANY, ANY, ANY], out_specs=(VMEM,) * 4,
            scratch_shapes=[whole, whole, whole, cols, moved, moved, pltpu.VMEM((2, 16, 128), bf16), pltpu.VMEM((2, 8, 128), jnp.int32), table, scaled, acc, dma(7)],
            name="plane_one",
        )(tile_cols, counts, scales, a_tiles, x, y)
        r1, r2, r3 = [move(p, slab_pairs(k)) for k, p in ((1, p1), (2, p2), (3, p3))]
        t1, t2, t3 = [move(q, slab_pairs(k, hubs)) for k, q in ((1, q1), (2, q2), (3, q3))]
        core = lax.axis_index("slab") % 2
        wide = lambda value: value.astype(f32)
        r1, r2, r3, mine = hold((r1, r2, r3, mine))
        theirs = move(mine, slab_pairs(1))
        same = kept2 + wide(r2)
        swapped = wide(r1) + wide(r3)
        own2 = jnp.where(core == 0, same, swapped)
        ahead2 = jnp.where(core == 0, swapped, same).astype(bf16)
        column, top, rest = pl.pallas_call(
            lambda *refs: panel_head(tile, *refs),
            out_shape=(shape((rows, half), f32), shape((half, rows), f32), shape((half, rows), f32)),
            in_specs=[SMEM] + [VMEM] * 4, out_specs=(VMEM, ANY, ANY),
            scratch_shapes=[pltpu.VMEM((rows, tile), f32), pltpu.VMEM((tile, rows), f32), pltpu.VMEM((tile, rows), f32),
                            dma(2)],
            name="panel_head",
        )(panel, keep, got, mine, theirs)
        t1, t2, t3, column, ahead2 = hold((t1, t2, t3, column, ahead2))
        ahead2 = move(ahead2, ahead_pairs)
        out1 = sum(wide(value[:rows]) for value in (kept1, t1, t2, t3))
        own1 = sum(wide(value[rows:]) for value in (kept1, t1, t2, t3))
        beside, ahead1, top = hold((out1.astype(bf16), own1.astype(bf16), top))
        beside = move(beside, beside_pairs)
        ahead1 = move(ahead1, even_ahead_pairs)
        column, lower = pl.pallas_call(
            lambda *refs: panel_tail(tile, *refs),
            out_shape=(shape((rows, half), f32), shape((tile, tile), bf16)),
            in_specs=[SMEM, ANY, ANY, ANY], out_specs=(ANY, ANY), input_output_aliases={3: 0},
            scratch_shapes=[pltpu.VMEM((tile, rows), f32), pltpu.VMEM((tile, rows), f32), pltpu.VMEM((tile, tile), bf16),
                            pltpu.VMEM((rows, half), f32), dma(2)],
            name="panel_tail",
            compiler_params=pltpu.CompilerParams(vmem_limit_bytes=64 * 2**20 - 2**16),
        )(panel, top, rest, column)
        lower = move(lower, slab_pairs(2))
        out = pl.pallas_call(
            lambda *refs: final_kernel(tile, *refs),
            out_shape=shape((3, rows, half), f32),
            in_specs=[VMEM] * 6, out_specs=VMEM, name="assemble",
            compiler_params=pltpu.CompilerParams(vmem_limit_bytes=64 * 2**20 - 2**16),
        )(column, own2, own1, ahead2, ahead1, beside)
        out = pl.pallas_call(
            lambda *refs: reduce_kernel(tile, *refs),
            out_shape=shape((3, rows, half), f32),
            in_specs=[SMEM, ANY, ANY], out_specs=ANY, input_output_aliases={2: 0},
            scratch_shapes=[pltpu.VMEM((tile, tile), bf16), pltpu.VMEM((tile, half), f32), dma(3)], name="reduce",
        )(panel, lower, out)
        return out.transpose(1, 0, 2)

    return body


def solution(mesh):
    return jax.shard_map(
        make_body(mesh.shape["blk"], mesh.shape["slab"]),
        mesh=mesh,
        in_specs=(P("blk", "slab"), P("blk", "slab", None), P("blk", "slab"), P("slab"), P()),
        out_specs=P("blk", None, "slab"),
        check_vma=False,
    )
```
